32 devices in a mesh: shot: 2 (over y), gx: 4 (over x, core), gy: 4 (over z).
Axes of the slice: x: 2, y: 2, z: 4, core: 2. Of those that a mesh axis runs over, the one named last changes fastest.
Arguments:
- src_p_prev: float32 [128, 64, 128], P(('shot', 'gx'), 'gy'), parts along dimension 0, may hold values from -6 to 6
- src_p_now: float32 [128, 64, 128], P(('shot', 'gx'), 'gy'), parts along dimension 0, may hold values from -6 to 6
- src_q_prev: float32 [128, 64, 128], P(('shot', 'gx'), 'gy'), parts along dimension 0, may hold values from -6 to 6
- src_q_now: float32 [128, 64, 128], P(('shot', 'gx'), 'gy'), parts along dimension 0, may hold values from -6 to 6
- rec_p_next: float32 [128, 64, 128], P(('shot', 'gx'), 'gy'), parts along dimension 0, may hold values from -6 to 6
- rec_p_now: float32 [128, 64, 128], P(('shot', 'gx'), 'gy'), parts along dimension 0, may hold values from -6 to 6
- rec_q_next: float32 [128, 64, 128], P(('shot', 'gx'), 'gy'), parts along dimension 0, may hold values from -6 to 6
- rec_q_now: float32 [128, 64, 128], P(('shot', 'gx'), 'gy'), parts along dimension 0, may hold values from -6 to 6
- velocity_term: float32 [64, 64, 128], P('gx', 'gy'), may hold values from 0.12 to 0.16
- epsilon: float32 [64, 64, 128], P('gx', 'gy'), may hold values from 0.2 to 0.4
- delta: float32 [64, 64, 128], P('gx', 'gy'), may hold values from 0 to 0.2
- tilt: float32 [64, 64, 128], P('gx', 'gy'), may hold values from 0 to 1.2
- azimuth: float32 [64, 64, 128], P('gx', 'gy'), may hold values from -3.140625 to 3.140625
- traces: float32 [32, 1024], P('shot', ('gx', 'gy')), parts along dimension 0, may hold values from -6 to 6
- receiver_x: int32 [1024], replicated, may hold values from 0 to 63
- receiver_y: int32 [1024], replicated, may hold values from 0 to 63
- segment_start: int32 [1], replicated, may hold values from 0 to 12
Outputs:
- image: float32 [128, 64, 128], P(('shot', 'gx'), 'gy'), parts along dimension 0
- rec_p_last: float32 [128, 64, 128], P(('shot', 'gx'), 'gy'), parts along dimension 0
- rec_q_last: float32 [128, 64, 128], P(('shot', 'gx'), 'gy'), parts along dimension 0
The draws below stay inside these ranges and needn't reach their ends.
There are 2 independent parts, one for each index of `shot`. The reference program is written for one: setup_inputs(seed, part) draws one part's arguments, and reference() takes and returns one part's arrays. A program takes and returns all parts, laid end to end along the dimension named above; an argument that names none is the same for every part. Nothing has to cross between parts.
All inputs are finite; a program needn't handle non-finite values.
Results may differ from the reference program's by a relative error of at most 0.00021.
Values sent between devices are 32-bit elements; how exact they have to be, the bound alone decides.
A program may use at most 64 MiB of HBM per device.

```python
import jax
import jax.numpy as jnp
from jax import lax

NZ = 128
STEPS = 4
NT = 16
REC_DEPTH = 4
NX = 64
NY = 64
NREC = 1024


def checker_field(key, salt):
    field_key = jax.random.fold_in(key, salt)
    noise_key = jax.random.fold_in(field_key, 0)
    row_index = lax.broadcasted_iota(jnp.int32, (NX, NY, NZ), 0)
    col_index = lax.broadcasted_iota(jnp.int32, (NX, NY, NZ), 1)
    sign_pattern = (1 - 2 * ((row_index + col_index) % 2)).astype(jnp.float32)
    noise = jax.random.normal(noise_key, (NX, NY, NZ), jnp.float32)
    amplitude = 1.0 + 0.6 * noise
    return jnp.clip(sign_pattern * amplitude, -6.0, 6.0)


def draw_src_p_prev(key, part):
    return checker_field(key, 101)


def draw_src_p_now(key, part):
    return checker_field(key, 102)


def draw_src_q_prev(key, part):
    return checker_field(key, 103)


def draw_src_q_now(key, part):
    return checker_field(key, 104)


def draw_rec_p_next(key, part):
    return checker_field(key, 105)


def draw_rec_p_now(key, part):
    return checker_field(key, 106)


def draw_rec_q_next(key, part):
    return checker_field(key, 107)


def draw_rec_q_now(key, part):
    return checker_field(key, 108)


def place_ends(result, stream_key, least, largest):
    place = [jax.random.randint(jax.random.fold_in(stream_key, axis), (), 0, length) for axis, length in enumerate(result.shape)]
    longest = result.shape.index(max(result.shape))
    neighbour = place[:longest] + [(place[longest] + 1) % result.shape[longest]] + place[longest + 1:]
    return result.at[tuple(place)].set(least).at[tuple(neighbour)].set(largest)


def levels(key, dims, pieces, least, high):
    gain, own = 1.0, jax.random.fold_in(key, 6)
    for position, parts in pieces:
        steps = jnp.exp(jax.random.uniform(jax.random.fold_in(own, position), (parts,), jnp.float32, least / len(pieces), high / len(pieces)))
        gain = gain * jnp.repeat(steps, dims[position] // parts).reshape([-1 if axis == position else 1 for axis in range(len(dims))])
    return gain


def gaussian(stream_key, shape, spread, limit, shards=(), held_as=jnp.bfloat16):
    drawn = jax.random.normal(stream_key, shape, jnp.float32) * spread
    if len(shards) > 0:
        drawn = levels(stream_key, shape, shards, -0.22, 0.18) * drawn
    return jnp.clip(drawn, min=-limit, max=limit).astype(held_as)


def setup_inputs(seed: int = 0, part: int = 0) -> dict:
    keys = jax.random.split(jax.random.key(seed), 18)
    own_keys = jax.random.split(jax.random.fold_in(keys[17], part), 18)
    src_p_prev = draw_src_p_prev(jax.random.fold_in(jax.random.fold_in(keys[17], part), 71), part)
    src_p_now = draw_src_p_now(jax.random.fold_in(jax.random.fold_in(keys[17], part), 71), part)
    src_q_prev = draw_src_q_prev(jax.random.fold_in(jax.random.fold_in(keys[17], part), 71), part)
    src_q_now = draw_src_q_now(jax.random.fold_in(jax.random.fold_in(keys[17], part), 71), part)
    rec_p_next = draw_rec_p_next(jax.random.fold_in(jax.random.fold_in(keys[17], part), 71), part)
    rec_p_now = draw_rec_p_now(jax.random.fold_in(jax.random.fold_in(keys[17], part), 71), part)
    rec_q_next = draw_rec_q_next(jax.random.fold_in(jax.random.fold_in(keys[17], part), 71), part)
    rec_q_now = draw_rec_q_now(jax.random.fold_in(jax.random.fold_in(keys[17], part), 71), part)
    velocity_term = jnp.clip(0.12 + 0.04 * jax.random.uniform(keys[8], (NX, NY, NZ), jnp.float32) ** levels(keys[8], (NX, NY, NZ), ((0, 4), (1, 4)), -0.2, 0.2), 0.12, 0.16)
    epsilon = jnp.clip(0.2 + 0.2 * jax.random.uniform(keys[9], (NX, NY, NZ), jnp.float32) ** levels(keys[9], (NX, NY, NZ), ((0, 4), (1, 4)), -0.2, 0.2), 0.2, 0.4)
    delta = jnp.clip(0.2 * jax.random.uniform(keys[10], (NX, NY, NZ), jnp.float32) ** levels(keys[10], (NX, NY, NZ), ((0, 4), (1, 4)), -0.2, 0.2), 0.0, 0.2)
    tilt = jnp.clip(1.2 * jax.random.uniform(keys[11], (NX, NY, NZ), jnp.float32) ** levels(keys[11], (NX, NY, NZ), ((0, 4), (1, 4)), -0.2, 0.2), 0.0, 1.2)
    azimuth = jnp.clip(jax.random.uniform(keys[12], (NX, NY, NZ), jnp.float32, -3.140625, 3.140625), -3.140625, 3.140625)
    traces = gaussian(own_keys[13], (NT, NREC), 1.0, 6.0, ((1, 16),), jnp.float32)
    receiver_x = place_ends(jax.random.randint(keys[14], (NREC,), 0, NX), jax.random.fold_in(keys[14], 1), 0, NX - 1).astype(jnp.int32)
    receiver_y = place_ends(jax.random.randint(keys[15], (NREC,), 0, NY), jax.random.fold_in(keys[15], 1), 0, NY - 1).astype(jnp.int32)
    segment_start = jax.random.randint(keys[16], (1,), 0, NT - STEPS + 1).astype(jnp.int32)
    return dict(src_p_prev=src_p_prev, src_p_now=src_p_now, src_q_prev=src_q_prev, src_q_now=src_q_now, rec_p_next=rec_p_next, rec_p_now=rec_p_now, rec_q_next=rec_q_next, rec_q_now=rec_q_now, velocity_term=velocity_term, epsilon=epsilon, delta=delta, tilt=tilt, azimuth=azimuth, traces=traces, receiver_x=receiver_x, receiver_y=receiver_y, segment_start=segment_start)


def factors_of(velocity_term, epsilon, delta, tilt, azimuth):
    sin_tilt = jnp.sin(tilt)
    cos_tilt = jnp.cos(tilt)
    sin_azim = jnp.sin(azimuth)
    cos_azim = jnp.cos(azimuth)
    sin_square = sin_tilt * sin_tilt
    double_tilt = 2.0 * sin_tilt * cos_tilt
    return (velocity_term, 1.0 + 2.0 * epsilon, jnp.sqrt(1.0 + 2.0 * delta), sin_square * cos_azim * cos_azim, sin_square * sin_azim * sin_azim, cos_tilt * cos_tilt, 2.0 * sin_square * sin_azim * cos_azim, double_tilt * cos_azim, double_tilt * sin_azim)

def rotated(padded, factors):
    center = padded[1:-1, 1:-1, 1:-1]
    d_xx = padded[2:, 1:-1, 1:-1] - 2.0 * center + padded[:-2, 1:-1, 1:-1]
    d_yy = padded[1:-1, 2:, 1:-1] - 2.0 * center + padded[1:-1, :-2, 1:-1]
    d_zz = padded[1:-1, 1:-1, 2:] - 2.0 * center + padded[1:-1, 1:-1, :-2]
    d_xy = 0.25 * (padded[2:, 2:, 1:-1] - padded[2:, :-2, 1:-1] - padded[:-2, 2:, 1:-1] + padded[:-2, :-2, 1:-1])
    d_xz = 0.25 * (padded[2:, 1:-1, 2:] - padded[2:, 1:-1, :-2] - padded[:-2, 1:-1, 2:] + padded[:-2, 1:-1, :-2])
    d_yz = 0.25 * (padded[1:-1, 2:, 2:] - padded[1:-1, 2:, :-2] - padded[1:-1, :-2, 2:] + padded[1:-1, :-2, :-2])
    along_axis = factors[3] * d_xx + factors[4] * d_yy + factors[5] * d_zz + factors[6] * d_xy + factors[7] * d_xz + factors[8] * d_yz
    return (along_axis, d_xx + d_yy + d_zz)

def advance(wave_state, factors):
    p_prev, p_now, q_prev, q_now = wave_state
    p_axis, p_laplace = rotated(jnp.pad(p_now, 1), factors)
    q_axis = rotated(jnp.pad(q_now, 1), factors)[0]
    p_across = p_laplace - p_axis
    p_next = 2.0 * p_now - p_prev + factors[0] * (factors[1] * p_across + factors[2] * q_axis)
    q_next = 2.0 * q_now - q_prev + factors[0] * (factors[2] * p_across + q_axis)
    return (p_next, q_next)

def reference(src_p_prev, src_p_now, src_q_prev, src_q_now, rec_p_next, rec_p_now, rec_q_next, rec_q_now, velocity_term, epsilon, delta, tilt, azimuth, traces, receiver_x, receiver_y, segment_start):
    factors = factors_of(velocity_term, epsilon, delta, tilt, azimuth)
    source_snaps = [src_p_now]
    wave_state = (src_p_prev, src_p_now, src_q_prev, src_q_now)
    for turn_index in range(STEPS):
        p_next, q_next = advance(wave_state, factors)
        wave_state = (wave_state[1], p_next, wave_state[3], q_next)
        source_snaps.append(p_next)
    window = lax.dynamic_slice_in_dim(traces, segment_start[0], STEPS, 0)
    image_sum = source_snaps[STEPS] * rec_p_now
    wave_state = (rec_p_next, rec_p_now, rec_q_next, rec_q_now)
    for turn_index in range(STEPS):
        sample = STEPS - 1 - turn_index
        p_next, q_next = advance(wave_state, factors)
        planes = jnp.zeros((NX, NY), jnp.float32).at[receiver_x, receiver_y].add(window[sample])
        p_next = p_next.at[:, :, REC_DEPTH].add(planes)
        wave_state = (wave_state[1], p_next, wave_state[3], q_next)
        image_sum = image_sum + source_snaps[sample] * p_next
    return (image_sum, wave_state[1], wave_state[3])
```

```python
import functools

import jax
import jax.numpy as jnp
from jax import lax
from jax.experimental import pallas as pl
from jax.experimental.pallas import tpu as pltpu
from jax.sharding import PartitionSpec as P

STEPS = 4
REC_DEPTH = 4
DEEP = 2
BASE = 8
TOP = 12
LANES = 128
SIDES = ((0, -1), (0, 1), (-1, 0), (1, 0), (-1, -1), (-1, 1), (1, -1), (1, 1))
MESH = pl.DeviceIdType.MESH
scope = jax.named_scope


def sine(x):
    s = x * x
    c = 1.6059044e-10
    for k in (-2.5052108e-8, 2.7557319e-6, -1.98412698e-4, 8.3333333e-3, -1.66666667e-1):
        c = c * s + k
    return x + x * (s * c)


def cosine(x):
    s = x * x
    c = -1.1470746e-11
    for k in (2.0876757e-9, -2.7557319e-7, 2.4801587e-5, -1.38888889e-3, 4.16666667e-2, -0.5):
        c = c * s + k
    return 1.0 + s * c


def kernel(sizes, *refs):
    n_gx, n_gy, nx, ny, nz, local_rec, n_rec = sizes
    fields, model = refs[:8], refs[8:13]
    traces, rec_x, rec_y, start = refs[13:17]
    image, p_last, q_last = refs[17:20]
    (*held, old_0, old_1, coef, earth, unit, inject, rows, window, gathered, rec_pos, pool,
     load_sem, send_sem, recv_sem) = refs[20:]
    waves = (held[:STEPS + 1], held[STEPS + 1:])
    olds = (old_0, old_1)
    wide = ny + 8
    n = n_gx * n_gy
    gx, gy = lax.axis_index("gx"), lax.axis_index("gy")
    me = gx * n_gy + gy

    barrier = pltpu.get_barrier_semaphore()

    def peer_id(i):
        peer = lax.rem(me + i, n)
        return {"gx": peer // n_gy, "gy": lax.rem(peer, n_gy)}

    def greet(i, carry):
        pl.semaphore_signal(barrier, inc=1, device_id=peer_id(i), device_id_type=MESH)
        return carry

    with scope("greet"):
        lax.fori_loop(1, n, greet, 0)

    def await_rows(sem, count):
        part = pool.at[pl.ds(0, count)]
        pltpu.make_async_copy(part, part, sem).wait()

    inner_x, inner_y = pl.ds(DEEP, nx), pl.ds(TOP, ny)

    with scope("loads"):
        for g in range(2):
            for f in range(2):
                pltpu.make_async_copy(
                    fields[4 * g + 2 * f + 1], waves[g][0].at[f, inner_x, inner_y], load_sem.at[0]
                ).start()
        for i in range(5):
            pltpu.make_async_copy(model[i], earth.at[i], load_sem.at[1]).start()
        load_traces = pltpu.make_async_copy(traces, rows, load_sem.at[2])
        load_traces.start()
        for g in range(2):
            for f in range(2):
                pltpu.make_async_copy(
                    fields[4 * g + 2 * f], olds[g].at[f, inner_x, inner_y], load_sem.at[3]
                ).start()
        load_x = pltpu.make_async_copy(rec_x, rec_pos.at[0], load_sem.at[4])
        load_y = pltpu.make_async_copy(rec_y, rec_pos.at[1], load_sem.at[5])
        load_x.start()
        load_y.start()

    def there(dx, dy):
        ok = None
        for d, pos, count in ((dx, gx, n_gx), (dy, gy, n_gy)):
            if d:
                test = pos + d < count if d > 0 else pos + d >= 0
                ok = test if ok is None else ok & test
        return ok

    def span(d, first, size, depth):
        if d == 0:
            return pl.ds(first, size), pl.ds(first, size)
        if d > 0:
            return pl.ds(first + size - depth, depth), pl.ds(first - depth, depth)
        return pl.ds(first, depth), pl.ds(first + size, depth)

    def send(ref, depth, slot, sides=SIDES):
        for dx, dy in sides:
            @pl.when(there(dx, dy))
            def _():
                src_x, dst_x = span(dx, DEEP, nx, depth)
                src_y, dst_y = span(dy, TOP, ny, depth)
                pltpu.make_async_remote_copy(
                    src_ref=ref.at[:, src_x, src_y],
                    dst_ref=ref.at[:, dst_x, dst_y],
                    send_sem=send_sem.at[0],
                    recv_sem=recv_sem.at[slot],
                    device_id={"gx": gx + dx, "gy": gy + dy},
                    device_id_type=MESH,
                ).start()

    def halo_rows(count, depth, beside_x, beside_y):
        return count * depth * (beside_x * ny + beside_y * nx + beside_x * beside_y * depth)

    def by_place(act):
        for beside_x in range(min(n_gx, 3)):
            for beside_y in range(min(n_gy, 3)):
                here_x = jnp.where(gx > 0, 1, 0) + jnp.where(gx < n_gx - 1, 1, 0) == beside_x
                here_y = jnp.where(gy > 0, 1, 0) + jnp.where(gy < n_gy - 1, 1, 0) == beside_y

                @pl.when(here_x & here_y)
                def _():
                    act(beside_x, beside_y)

    def await_halo(count, depth, slot):
        def act(beside_x, beside_y):
            total = halo_rows(count, depth, beside_x, beside_y)
            if total:
                await_rows(recv_sem.at[slot], total)

        by_place(act)

    with scope("wait_now"):
        await_rows(load_sem.at[0], 4 * nx * ny)
    with scope("barrier"):
        pl.semaphore_wait(barrier, n - 1)
    with scope("send_src_now"):
        send(waves[0][0], DEEP, 0)

    with scope("wait_model"):
        await_rows(load_sem.at[1], 5 * nx * ny)

    def units(x, carry):
        v = earth[0, x]
        f_e = 1.0 + 2.0 * earth[1, x]
        f_d = jnp.sqrt(1.0 + 2.0 * earth[2, x])
        tilt = earth[3, x]
        half = 0.5 * earth[4, x]
        sin_t, cos_t = sine(tilt), cosine(tilt)
        sin_h, cos_h = sine(half), cosine(half)
        sin_a = 2.0 * sin_h * cos_h
        cos_a = 1.0 - 2.0 * sin_h * sin_h
        to = (x + DEEP, inner_y)
        unit[(0, *to)] = v
        unit[(1, *to)] = v * f_e
        unit[(2, *to)] = v * f_d
        unit[(3, *to)] = sin_t * cos_a
        unit[(4, *to)] = sin_t * sin_a
        unit[(5, *to)] = cos_t
        return carry

    with scope("units"):
        lax.fori_loop(0, nx, units, 0, unroll=4)
    with scope("send_model"):
        send(unit, 1, 1)

    with scope("wait_prev"):
        await_rows(load_sem.at[3], 4 * nx * ny)
    with scope("send_src_prev"):
        send(olds[0], 1, 2)

    with scope("window"):
        load_traces.wait()
        window[...] = jnp.zeros_like(window)
        window[0:STEPS, 0:local_rec] = rows[pl.ds(start[0], STEPS), :]
        gathered[me] = window[...]

    def far_start(i, carry):
        pltpu.make_async_remote_copy(
            src_ref=window,
            dst_ref=gathered.at[me],
            send_sem=send_sem.at[0],
            recv_sem=recv_sem.at[7],
            device_id=peer_id(i),
            device_id_type=MESH,
        ).start()
        return carry

    with scope("far_start"):
        lax.fori_loop(1, n, far_start, 0)
    with scope("send_rec"):
        send(waves[1][0], DEEP, 3)
        send(olds[1], 1, 4)

    def clear(ref, count, depth):
        zeros = jnp.zeros((wide, nz), jnp.float32)
        for edge, first in ((gx == 0, DEEP - depth), (gx == n_gx - 1, DEEP + nx)):
            @pl.when(edge)
            def _():
                for f in range(count):
                    for x in range(first, first + depth):
                        ref[f, x, BASE:BASE + wide] = zeros
        for edge, first in ((gy == 0, TOP - depth), (gy == n_gy - 1, TOP + ny)):
            @pl.when(edge)
            def _():
                for f in range(count):
                    ref[f, :, first:first + depth] = jnp.zeros((nx + 2 * DEEP, depth, nz), jnp.float32)

    with scope("clear"):
        for g in range(2):
            clear(waves[g][0], 2, DEEP)
            clear(waves[g][2], 2, DEEP)
            clear(olds[g], 2, 1)
        clear(unit, 6, 1)

    def after(value):
        return pltpu.roll(value, nz - 1, 1)

    def before(value):
        return pltpu.roll(value, 1, 1)

    def factors(x, first, count):
        lane = lax.broadcasted_iota(jnp.int32, (count, nz), 1)
        at = pl.ds(first, count)
        to = pl.ds(first - BASE, count)
        n_x, n_y, n_z = unit[3, x, at], unit[4, x, at], unit[5, x, at]
        a_xx, a_yy, a_zz = n_x * n_x, n_y * n_y, n_z * n_z
        half_z = 0.5 * n_z
        a_xz, a_yz = half_z * n_x, half_z * n_y
        coef[0, x, to] = a_xx
        coef[1, x, to] = a_yy
        coef[4, x, to] = 1.0 - a_xx
        coef[5, x, to] = 1.0 - a_yy
        coef[8, x, to] = (0.5 * n_x) * n_y
        for shift, edge, i in ((before, lane == 0, 0), (after, lane == nz - 1, 1)):
            moved = shift(a_zz)
            coef[2 + i, x, to] = jnp.where(edge, 0.0, moved)
            coef[6 + i, x, to] = jnp.where(edge, 0.0, 1.0 - moved)
            coef[9 + 2 * i, x, to] = jnp.where(edge, 0.0, shift(a_xz))
            coef[10 + 2 * i, x, to] = jnp.where(edge, 0.0, shift(a_yz))

    def inner_factors(x, carry):
        factors(x, BASE + 8, wide - 16)
        return carry

    def outer_factors(x, carry):
        factors(x, BASE, 8)
        factors(x, BASE + wide - 8, 8)
        return carry

    with scope("inner_factors"):
        lax.fori_loop(DEEP, DEEP + nx, inner_factors, 0, unroll=4)

    load_x.wait()
    load_y.wait()

    def rotated(now, f, x, lo, count, center, weights):
        sign, w_x, w_y, w_up, w_down = weights
        mid, up, down = pl.ds(lo, count), pl.ds(lo + 1, count), pl.ds(lo - 1, count)
        at = pl.ds(lo - BASE, count)
        x_up, x_down = now[f, x + 1, mid], now[f, x - 1, mid]
        y_up, y_down = now[f, x, up], now[f, x, down]
        d_x, d_y = x_up - x_down, y_up - y_down
        d_xy = (now[f, x + 1, up] - now[f, x + 1, down]) - (now[f, x - 1, up] - now[f, x - 1, down])
        flat = coef[w_x, x, at] * (x_up + x_down) + coef[w_y, x, at] * (y_up + y_down)
        mixed = coef[8, x, at] * d_xy
        above, below = coef[w_up, x, at] * center, coef[w_down, x, at] * center
        mixed_above = coef[9, x, at] * d_x + coef[10, x, at] * d_y
        mixed_below = coef[11, x, at] * d_x + coef[12, x, at] * d_y
        if sign > 0:
            return (flat + mixed) + (after(above + mixed_above) + before(below - mixed_below))
        return (flat - mixed) + (after(above - mixed_above) + before(below + mixed_below))

    def step(g, level):
        now = waves[g][level]
        prev = waves[g][level - 1] if level else olds[g]
        ring = 1 - level % 2
        lo, count = (BASE, wide) if ring else (TOP, ny)
        mid = pl.ds(lo, count)

        def plane(x, carry):
            p_now, q_now = now[0, x, mid], now[1, x, mid]
            p_two, q_two = p_now + p_now, q_now + q_now
            across = rotated(now, 0, x, lo, count, p_now, (-1, 4, 5, 6, 7)) - (p_two + p_two)
            q_axis = rotated(now, 1, x, lo, count, q_now, (1, 0, 1, 2, 3)) - q_two
            v_d = unit[2, x, mid]
            p_next = (p_two - prev[0, x, mid]) + (unit[1, x, mid] * across + v_d * q_axis)
            if g == 1:
                p_next = p_next + inject[STEPS - 1 - level, x, pl.ds(lo - BASE, count)]
            if g == 0 and level == STEPS - 1:
                waves[g][level + 1][0, x, mid] = p_next
                return carry
            q_next = (q_two - prev[1, x, mid]) + (v_d * across + unit[0, x, mid] * q_axis)
            if g == 1 and level == STEPS - 1:
                p_last[x - DEEP] = p_next
                q_last[x - DEEP] = q_next
                total = waves[0][0][0, x, mid] * p_next
                for k in range(STEPS):
                    total = total + waves[1][k][0, x, mid] * waves[0][STEPS - k][0, x, mid]
                image[x - DEEP] = total
            else:
                waves[g][level + 1][0, x, mid] = p_next
                waves[g][level + 1][1, x, mid] = q_next
            return carry

        lax.fori_loop(DEEP - ring, DEEP + nx + ring, plane, 0, unroll=(nx + 2 * ring) // 2)

    def make_planes():
        per_row = LANES // local_rec
        n_rows = n_rec // LANES
        chunk = min(8, n_rows)
        wide_x = (nx + 2 + 7) // 8 * 8
        x_id = lax.broadcasted_iota(jnp.int32, (wide_x, LANES), 0) + (gx * nx - 1)
        y_id = lax.broadcasted_iota(jnp.int32, (wide, LANES), 0) + (gy * ny - (TOP - BASE))
        total = jnp.zeros((wide, STEPS * wide_x), jnp.float32)
        for base in range(0, n_rows, chunk):
            lefts, rights = [], []
            for i in range(base, base + chunk):
                sample = gathered[i * per_row]
                for j in range(1, per_row):
                    sample = sample + pltpu.roll(gathered[i * per_row + j], j * local_rec, 1)
                at_x = rec_pos[0, i:i + 1] == x_id
                lefts.append(jnp.where(rec_pos[1, i:i + 1] == y_id, 1.0, 0.0))
                rights.append(
                    jnp.concatenate(
                        [jnp.where(at_x, sample[k:k + 1], 0.0) for k in range(STEPS)], axis=0
                    )
                )
            total = total + lax.dot_general(
                jnp.concatenate(lefts, axis=1),
                jnp.concatenate(rights, axis=1),
                (((1,), (1,)), ((), ())),
                precision=lax.Precision.HIGHEST,
                preferred_element_type=jnp.float32,
            )
        here = lax.broadcasted_iota(jnp.int32, (wide, nz), 1) == REC_DEPTH
        for k in range(STEPS):
            for x in range(nx + 2):
                column = k * wide_x + x
                inject[k, DEEP - 1 + x] = jnp.where(here, total[:, column:column + 1], 0.0)

    with scope("wait_model_halo"):
        await_halo(6, 1, 1)
    with scope("outer_factors"):
        lax.fori_loop(DEEP, DEEP + nx, outer_factors, 0, unroll=4)
        for x in (DEEP - 1, DEEP + nx):
            factors(x, BASE, wide)
    with scope("wait_src0"):
        await_halo(2, DEEP, 0)
        await_halo(2, 1, 2)
    with scope("src_step0"):
        step(0, 0)
    with scope("src_step1"):
        step(0, 1)
    with scope("send_src2"):
        send(waves[0][2], DEEP, 5)
    with scope("wait_far"):
        if n > 1:
            await_rows(recv_sem.at[7], 8 * (n - 1))
    with scope("planes"):
        make_planes()
    with scope("wait_rec0"):
        await_halo(2, DEEP, 3)
        await_halo(2, 1, 4)
    with scope("rec_step0"):
        step(1, 0)
    with scope("rec_step1"):
        step(1, 1)
    with scope("send_rec2"):
        send(waves[1][2], DEEP, 6)
    with scope("wait_src2"):
        await_halo(2, DEEP, 5)
    with scope("src_step2"):
        step(0, 2)
    with scope("src_step3"):
        step(0, 3)
    with scope("wait_rec2"):
        await_halo(2, DEEP, 6)
    with scope("rec_step2"):
        step(1, 2)
    with scope("rec_step3"):
        step(1, 3)

    def finish(beside_x, beside_y):
        total = 8 * (n - 1)
        for count, depth in ((8, DEEP), (6, 1), (4, 1)):
            total += halo_rows(count, depth, beside_x, beside_y)
        if total:
            await_rows(send_sem.at[0], total)

    with scope("finish"):
        by_place(finish)


def write_out(*refs):
    values, results, done = refs[:3], refs[3:6], refs[6]
    copies = [pltpu.make_async_copy(values[i], results[i], done.at[i]) for i in range(3)]
    for copy in copies:
        copy.start()
    for copy in copies:
        copy.wait()


def per_device(*args):
    nx, ny, nz = args[0].shape
    n_gx, n_gy = lax.axis_size("gx"), lax.axis_size("gy")
    traces, receiver_x, receiver_y, segment_start = args[13:]
    samples, local_rec = traces.shape
    n_rec = receiver_x.shape[0]
    n = n_gx * n_gy
    sizes = (n_gx, n_gy, nx, ny, nz, local_rec, n_rec)
    positions = [r.reshape(n_rec // LANES, LANES) for r in (receiver_x, receiver_y)]
    anywhere = pl.BlockSpec(memory_space=pltpu.HBM)
    block = jax.ShapeDtypeStruct((nx, ny, nz), jnp.float32)
    held = pltpu.VMEM((nx, ny, nz), jnp.float32)
    ends = pl.pallas_call(
        functools.partial(kernel, sizes),
        out_shape=(held,) * 3,
        in_specs=[anywhere] * 16 + [pl.BlockSpec(memory_space=pltpu.SMEM)],
        out_specs=(pl.BlockSpec(memory_space=pltpu.VMEM),) * 3,
        scratch_shapes=[
            *[pltpu.VMEM((2, nx + 2 * DEEP, ny + 2 * TOP, nz), jnp.float32)] * (2 * STEPS + 4),
            pltpu.VMEM((13, nx + 2 * DEEP, ny + 8, nz), jnp.float32),
            pltpu.VMEM((5, nx, ny, nz), jnp.float32),
            pltpu.VMEM((6, nx + 2 * DEEP, ny + 2 * TOP, nz), jnp.float32),
            pltpu.VMEM((STEPS, nx + 2 * DEEP, ny + 8, nz), jnp.float32),
            pltpu.VMEM((samples, local_rec), jnp.float32),
            pltpu.VMEM((8, LANES), jnp.float32),
            pltpu.VMEM((n, 8, LANES), jnp.float32),
            pltpu.VMEM((2, n_rec // LANES, LANES), jnp.int32),
            pltpu.VMEM((16 * n + 24 * (nx + 4) * (ny + 4), LANES), jnp.float32),
            pltpu.SemaphoreType.DMA((6,)),
            pltpu.SemaphoreType.DMA((1,)),
            pltpu.SemaphoreType.DMA((8,)),
        ],
        compiler_params=pltpu.CompilerParams(
            collective_id=0, has_side_effects=True, vmem_limit_bytes=48 * 1024 * 1024
        ),
        name="window",
    )(*[pltpu.with_memory_space_constraint(a, pltpu.HBM) for a in (*args[:13], traces, *positions)], segment_start)
    return pl.pallas_call(
        write_out,
        out_shape=(block,) * 3,
        in_specs=[pl.BlockSpec(memory_space=pltpu.VMEM)] * 3,
        out_specs=(pl.BlockSpec(memory_space=pltpu.HBM),) * 3,
        scratch_shapes=[pltpu.SemaphoreType.DMA((3,))],
        compiler_params=pltpu.CompilerParams(vmem_limit_bytes=1024 * 1024),
        name="write_out",
    )(*[pltpu.with_memory_space_constraint(end, pltpu.VMEM) for end in ends])


def solution(mesh):
    block, cell = P(("shot", "gx"), "gy", None), P("gx", "gy", None)
    return jax.shard_map(
        per_device,
        mesh=mesh,
        in_specs=(block,) * 8 + (cell,) * 5 + (P("shot", ("gx", "gy")), P(), P(), P()),
        out_specs=(block,) * 3,
        check_vma=False,
    )
```

```python
import functools

import jax
import jax.numpy as jnp
from jax import lax
from jax.experimental import pallas as pl
from jax.experimental.pallas import tpu as pltpu
from jax.sharding import PartitionSpec as P

STEPS = 4
REC_DEPTH = 4
DEEP = 3
RINGS = (0, 2, 1, 0)
BASE = 8
TOP = 12
LANES = 128
SIDES = ((0, -1), (0, 1), (-1, 0), (1, 0), (-1, -1), (-1, 1), (1, -1), (1, 1))
MESH = pl.DeviceIdType.MESH
scope = jax.named_scope


def sine(x):
    s = x * x
    c = 1.6059044e-10
    for k in (-2.5052108e-8, 2.7557319e-6, -1.98412698e-4, 8.3333333e-3, -1.66666667e-1):
        c = c * s + k
    return x + x * (s * c)


def cosine(x):
    s = x * x
    c = -1.1470746e-11
    for k in (2.0876757e-9, -2.7557319e-7, 2.4801587e-5, -1.38888889e-3, 4.16666667e-2, -0.5):
        c = c * s + k
    return 1.0 + s * c


def kernel(sizes, *refs):
    n_gx, n_gy, nx, ny, nz, local_rec, n_rec = sizes
    fields, model = refs[:8], refs[8:13]
    traces, rec_x, rec_y, start = refs[13:17]
    image, p_last, q_last = refs[17:20]
    (*held, old_0, old_1, coef, earth, unit, inject, rows, window, gathered, rec_pos, hot_x, hot_y, pool,
     load_sem, send_sem, recv_sem) = refs[20:]
    waves = (held[:STEPS + 1], held[STEPS + 1:])
    olds = (old_0, old_1)
    wide = ny + 8
    n = n_gx * n_gy
    gx, gy = lax.axis_index("gx"), lax.axis_index("gy")
    me = gx * n_gy + gy

    barrier = pltpu.get_barrier_semaphore()

    def peer_id(i):
        peer = lax.rem(me + i, n)
        return {"gx": peer // n_gy, "gy": lax.rem(peer, n_gy)}

    def greet(i, carry):
        pl.semaphore_signal(barrier, inc=1, device_id=peer_id(i), device_id_type=MESH)
        return carry

    def await_rows(sem, count):
        part = pool.at[pl.ds(0, count)]
        pltpu.make_async_copy(part, part, sem).wait()

    inner_x, inner_y = pl.ds(DEEP, nx), pl.ds(TOP, ny)

    with scope("loads"):
        for i in range(5):
            pltpu.make_async_copy(model[i], earth.at[i], load_sem.at[1]).start()
        for g in range(2):
            for f in range(2):
                pltpu.make_async_copy(
                    fields[4 * g + 2 * f + 1], waves[g][0].at[f, inner_x, inner_y], load_sem.at[0]
                ).start()
        load_traces = pltpu.make_async_copy(traces, rows, load_sem.at[2])
        load_traces.start()

    with scope("greet"):
        lax.fori_loop(1, n, greet, 0)

    def there(dx, dy):
        ok = None
        for d, pos, count in ((dx, gx, n_gx), (dy, gy, n_gy)):
            if d:
                test = pos + d < count if d > 0 else pos + d >= 0
                ok = test if ok is None else ok & test
        return ok

    def span(d, start, size, first, last):
        if d == 0:
            return pl.ds(start, size), pl.ds(start, size)
        if d > 0:
            return pl.ds(start + size - last, last - first), pl.ds(start - last, last - first)
        return pl.ds(start + first, last - first), pl.ds(start + size + first, last - first)

    def send(ref, slot, near, far, corner, out=0):
        for dx, dy in SIDES:
            first, last = (0, corner) if dx and dy else (near, far)
            if last == first:
                continue

            @pl.when(there(dx, dy))
            def _():
                src_x, dst_x = span(dx, DEEP, nx, first, last)
                src_y, dst_y = span(dy, TOP, ny, first, last)
                pltpu.make_async_remote_copy(
                    src_ref=ref.at[:, src_x, src_y],
                    dst_ref=ref.at[:, dst_x, dst_y],
                    send_sem=send_sem.at[out],
                    recv_sem=recv_sem.at[slot],
                    device_id={"gx": gx + dx, "gy": gy + dy},
                    device_id_type=MESH,
                ).start()

    def halo_rows(count, layers, corner, beside_x, beside_y):
        faces = beside_x * ny + beside_y * nx
        return count * (layers * faces + beside_x * beside_y * corner * corner)

    def by_place(act):
        for beside_x in range(min(n_gx, 3)):
            for beside_y in range(min(n_gy, 3)):
                here_x = jnp.where(gx > 0, 1, 0) + jnp.where(gx < n_gx - 1, 1, 0) == beside_x
                here_y = jnp.where(gy > 0, 1, 0) + jnp.where(gy < n_gy - 1, 1, 0) == beside_y

                @pl.when(here_x & here_y)
                def _():
                    act(beside_x, beside_y)

    def await_halo(slot, *groups, sems=recv_sem):
        def act(beside_x, beside_y):
            total = sum(halo_rows(*group, beside_x, beside_y) for group in groups)
            if total:
                await_rows(sems.at[slot], total)

        by_place(act)

    with scope("wait_model"):
        await_rows(load_sem.at[1], 5 * nx * ny)

    def units(x, carry):
        v = earth[0, x]
        f_e = 1.0 + 2.0 * earth[1, x]
        f_d = jnp.sqrt(1.0 + 2.0 * earth[2, x])
        tilt = earth[3, x]
        half = 0.5 * earth[4, x]
        sin_t = sine(tilt)
        sin_h, cos_h = sine(half), cosine(half)
        sin_a = 2.0 * sin_h * cos_h
        cos_a = 1.0 - 2.0 * sin_h * sin_h
        to = (x + DEEP, inner_y)
        unit[(0, *to)] = v
        unit[(1, *to)] = v * f_e
        unit[(2, *to)] = v * f_d
        unit[(3, *to)] = sin_t * cos_a
        unit[(4, *to)] = sin_t * sin_a
        return carry

    with scope("units"):
        lax.fori_loop(0, nx, units, 0, unroll=nx)
    with scope("wait_now"):
        await_rows(load_sem.at[0], 4 * nx * ny)
    with scope("barrier"):
        pl.semaphore_wait(barrier, n - 1)
    with scope("send_now"):
        send(waves[0][0], 0, 0, 1, 2)
        send(waves[1][0], 1, 0, 1, 2)

    per_row = LANES // local_rec
    packed = STEPS // per_row
    with scope("window"):
        load_traces.wait()
        window[...] = jnp.zeros_like(window)
        window[0:STEPS, 0:local_rec] = rows[pl.ds(start[0], STEPS), :]
        sample = window[...]
        for r in range(packed):
            row = sample[r * per_row:r * per_row + 1]
            for j in range(1, per_row):
                row = row + pltpu.roll(sample[r * per_row + j:r * per_row + j + 1], j * local_rec, 1)
            window[r:r + 1] = row
        mine = pl.ds(pl.multiple_of(me * 8, 8), packed)
        gathered[mine] = window[0:packed]

    def far_start(i, carry):
        pltpu.make_async_remote_copy(
            src_ref=window.at[0:packed],
            dst_ref=gathered.at[mine],
            send_sem=send_sem.at[0],
            recv_sem=recv_sem.at[7],
            device_id=peer_id(i),
            device_id_type=MESH,
        ).start()
        return carry

    with scope("far_start"):
        lax.fori_loop(1, n, far_start, 0)

    with scope("send_model"):
        send(unit, 2, 0, 2, 2)
    with scope("send_layer"):
        send(waves[0][0], 3, 1, 2, 0)
        send(waves[1][0], 3, 1, 2, 0)
    for g in range(2):
        for f in range(2):
            pltpu.make_async_copy(
                fields[4 * g + 2 * f], olds[g].at[f, :, pl.ds(TOP - BASE, ny)], load_sem.at[3]
            ).start()
    load_x = pltpu.make_async_copy(rec_x, rec_pos.at[0], load_sem.at[4])
    load_y = pltpu.make_async_copy(rec_y, rec_pos.at[1], load_sem.at[5])
    load_x.start()
    load_y.start()

    def clear(ref, count, depth):
        zeros = jnp.zeros((wide, nz), jnp.float32)
        for edge, first in ((gx == 0, DEEP - depth), (gx == n_gx - 1, DEEP + nx)):
            @pl.when(edge)
            def _():
                for f in range(count):
                    for x in range(first, first + depth):
                        ref[f, x, BASE:BASE + wide] = zeros
        for edge, first in ((gy == 0, TOP - depth), (gy == n_gy - 1, TOP + ny)):
            @pl.when(edge)
            def _():
                for f in range(count):
                    ref[f, :, first:first + depth] = jnp.zeros((nx + 2 * DEEP, depth, nz), jnp.float32)

    with scope("clear"):
        for g in range(2):
            clear(waves[g][0], 2, 2)
            clear(waves[g][1], 2, 3)
        clear(unit, 5, 2)

    def after(value):
        return pltpu.roll(value, nz - 1, 1)

    def before(value):
        return pltpu.roll(value, 1, 1)

    def factors(x, first, count):
        lane = lax.broadcasted_iota(jnp.int32, (count, nz), 1)
        at = pl.ds(first, count)
        to = pl.ds(first - BASE, count)
        n_x, n_y = unit[3, x, at], unit[4, x, at]
        a_xx, a_yy = n_x * n_x, n_y * n_y
        a_zz = 1.0 - (a_xx + a_yy)
        half_z = 0.5 * jnp.sqrt(a_zz)
        a_xz, a_yz = half_z * n_x, half_z * n_y
        coef[0, x, to] = a_xx
        coef[1, x, to] = a_yy
        coef[4, x, to] = 1.0 - a_xx
        coef[5, x, to] = 1.0 - a_yy
        coef[8, x, to] = (0.5 * n_x) * n_y
        for shift, edge, i in ((before, lane == 0, 0), (after, lane == nz - 1, 1)):
            moved = shift(a_zz)
            coef[2 + i, x, to] = jnp.where(edge, 0.0, moved)
            coef[6 + i, x, to] = jnp.where(edge, 0.0, 1.0 - moved)
            coef[9 + 2 * i, x, to] = jnp.where(edge, 0.0, shift(a_xz))
            coef[10 + 2 * i, x, to] = jnp.where(edge, 0.0, shift(a_yz))

    def inner_factors(x, carry):
        factors(x, TOP, ny)
        return carry

    def outer_factors(x, carry):
        factors(x, BASE, 8)
        factors(x, BASE + wide - 8, 8)
        return carry

    with scope("inner_factors"):
        lax.fori_loop(DEEP, DEEP + nx, inner_factors, 0, unroll=nx)

    def rotated(now, f, x, lo, count, center, weights):
        sign, w_x, w_y, w_up, w_down = weights
        mid, up, down = pl.ds(lo, count), pl.ds(lo + 1, count), pl.ds(lo - 1, count)
        at = pl.ds(lo - BASE, count)
        x_up, x_down = now[f, x + 1, mid], now[f, x - 1, mid]
        y_up, y_down = now[f, x, up], now[f, x, down]
        d_x, d_y = x_up - x_down, y_up - y_down
        d_xy = (now[f, x + 1, up] - now[f, x + 1, down]) - (now[f, x - 1, up] - now[f, x - 1, down])
        flat = coef[w_x, x, at] * (x_up + x_down) + coef[w_y, x, at] * (y_up + y_down)
        mixed = coef[8, x, at] * d_xy
        above, below = coef[w_up, x, at] * center, coef[w_down, x, at] * center
        mixed_above = coef[9, x, at] * d_x + coef[10, x, at] * d_y
        mixed_below = coef[11, x, at] * d_x + coef[12, x, at] * d_y
        if sign > 0:
            return (flat + mixed) + (after(above + mixed_above) + before(below - mixed_below))
        return (flat - mixed) + (after(above - mixed_above) + before(below + mixed_below))

    def step(g, level):
        now = waves[g][level]
        ring = RINGS[level]
        lo, count = (BASE, wide) if ring else (TOP, ny)
        mid = pl.ds(lo, count)

        def plane(x, carry):
            p_now, q_now = now[0, x, mid], now[1, x, mid]
            p_two, q_two = p_now + p_now, q_now + q_now
            across = rotated(now, 0, x, lo, count, p_now, (-1, 4, 5, 6, 7)) - (p_two + p_two)
            q_axis = rotated(now, 1, x, lo, count, q_now, (1, 0, 1, 2, 3)) - q_two
            v_d = unit[2, x, mid]
            if level:
                p_prev, q_prev = waves[g][level - 1][0, x, mid], waves[g][level - 1][1, x, mid]
            else:
                p_prev, q_prev = olds[g][0, x - DEEP, TOP - BASE:TOP - BASE + ny], olds[g][1, x - DEEP, TOP - BASE:TOP - BASE + ny]
            p_next = (p_two - p_prev) + (unit[1, x, mid] * across + v_d * q_axis)
            if g == 1 and level:
                p_next = p_next + inject[STEPS - 1 - level, x, pl.ds(lo - BASE, count)]
            if g == 0 and level == STEPS - 1:
                waves[g][level + 1][0, x, mid] = p_next
                return carry
            q_next = (q_two - q_prev) + (v_d * across + unit[0, x, mid] * q_axis)
            if g == 1 and level == STEPS - 1:
                p_last[x - DEEP] = p_next
                q_last[x - DEEP] = q_next
                total = waves[0][0][0, x, mid] * p_next
                for k in range(STEPS):
                    total = total + waves[1][k][0, x, mid] * waves[0][STEPS - k][0, x, mid]
                image[x - DEEP] = total
            else:
                waves[g][level + 1][0, x, mid] = p_next
                waves[g][level + 1][1, x, mid] = q_next
            return carry

        lax.fori_loop(DEEP - ring, DEEP + nx + ring, plane, 0, unroll=nx + 2 * ring)

    n_rows = n_rec // LANES
    wide_x = hot_x.shape[0]

    def find(i, carry):
        to = pl.ds(pl.multiple_of(i * LANES, LANES), LANES)
        x_id = lax.broadcasted_iota(jnp.int32, (wide_x, LANES), 0) + (gx * nx - DEEP)
        y_id = lax.broadcasted_iota(jnp.int32, (wide, LANES), 0) + (gy * ny - (TOP - BASE))
        hot_x[:, to] = jnp.where(rec_pos[0, pl.ds(i, 1)] == x_id, 1.0, 0.0)
        hot_y[:, to] = jnp.where(rec_pos[1, pl.ds(i, 1)] == y_id, 1.0, 0.0)
        return carry

    with scope("find"):
        load_x.wait()
        load_y.wait()
        lax.fori_loop(0, n_rows, find, 0, unroll=8)

    def make_planes():
        segment = lax.broadcasted_iota(jnp.int32, (n_rows, LANES), 1) // local_rec
        parts = []
        for k in range(STEPS):
            r, own = k // per_row, k % per_row
            sample = None
            for j in range(per_row):
                piece = gathered[pl.ds(j * 8 + r, n_rows, stride=per_row * 8), :]
                piece = jnp.where(segment == own, piece, 0.0)
                if j != own:
                    piece = pltpu.roll(piece, (j - own) * local_rec % LANES, 1)
                sample = piece if sample is None else sample + piece
            for _ in range(3):
                part = sample.astype(jnp.bfloat16).astype(jnp.float32)
                parts.append(part)
                sample = sample - part
        chunk = min(8, n_rows)
        total = jnp.zeros((3 * STEPS * wide, wide_x), jnp.float32)
        for base in range(0, n_rows, chunk):
            columns = slice(base * LANES, (base + chunk) * LANES)
            left = jnp.concatenate(
                [
                    jnp.concatenate(
                        [hot_y[:, i * LANES:(i + 1) * LANES] * part[i:i + 1] for part in parts], axis=0
                    )
                    for i in range(base, base + chunk)
                ],
                axis=1,
            )
            total = total + lax.dot_general(
                left, hot_x[:, columns], (((1,), (1,)), ((), ())), preferred_element_type=jnp.float32
            )
        here = lax.broadcasted_iota(jnp.int32, (wide, nz), 1) == REC_DEPTH
        for k in range(STEPS):
            three = [total[(3 * k + i) * wide:(3 * k + i + 1) * wide] for i in range(3)]
            plane = (three[0] + three[1]) + three[2]
            for x in range(nx + 2 * DEEP):
                inject[k, x] = jnp.where(here, plane[:, x:x + 1], 0.0)

    with scope("wait_prev"):
        await_rows(load_sem.at[3], 4 * nx * ny)
    with scope("wait_src0"):
        await_halo(0, (2, 1, 2))
    with scope("src_step0"):
        step(0, 0)
    with scope("send_src1"):
        send(waves[0][1], 5, 0, 3, 3)
    with scope("wait_rec0"):
        await_halo(1, (2, 1, 2))
    with scope("rec_step0"):
        step(1, 0)
    with scope("send_rec1"):
        send(waves[1][1], 6, 0, 3, 3, out=1)
    with scope("wait_far"):
        if n > 1:
            await_rows(recv_sem.at[7], packed * (n - 1))
    with scope("planes"):
        make_planes()
    with scope("wait_model_halo"):
        await_halo(2, (5, 2, 2))
    with scope("outer_factors"):
        lax.fori_loop(DEEP, DEEP + nx, outer_factors, 0, unroll=nx)
        for x in (DEEP - 2, DEEP - 1, DEEP + nx, DEEP + nx + 1):
            factors(x, BASE, wide)
    with scope("wait_src1"):
        await_halo(3, (4, 1, 0))
        await_halo(5, (2, 3, 3))
    for level in range(1, STEPS):
        with scope("src_step%d" % level):
            step(0, level)
    with scope("wait_rec1"):
        await_halo(6, (2, 3, 3))
        await_halo(1, (2, 3, 3), sems=send_sem)

    def add_samples(x, carry):
        ext = pl.ds(BASE, wide)
        waves[1][1][0, x, ext] = waves[1][1][0, x, ext] + inject[STEPS - 1, x]
        return carry

    with scope("add_samples"):
        lax.fori_loop(0, nx + 2 * DEEP, add_samples, 0, unroll=nx + 2 * DEEP)
    for level in range(1, STEPS):
        with scope("rec_step%d" % level):
            step(1, level)

    def finish(beside_x, beside_y):
        total = packed * (n - 1)
        for group in ((4, 1, 2), (5, 2, 2), (4, 1, 0), (2, 3, 3)):
            total += halo_rows(*group, beside_x, beside_y)
        if total:
            await_rows(send_sem.at[0], total)

    with scope("finish"):
        by_place(finish)


def write_out(*refs):
    values, results, done = refs[:3], refs[3:6], refs[6]
    copies = [pltpu.make_async_copy(values[i], results[i], done.at[i]) for i in range(3)]
    for copy in copies:
        copy.start()
    for copy in copies:
        copy.wait()


def per_device(*args):
    nx, ny, nz = args[0].shape
    n_gx, n_gy = lax.axis_size("gx"), lax.axis_size("gy")
    traces, receiver_x, receiver_y, segment_start = args[13:]
    samples, local_rec = traces.shape
    n_rec = receiver_x.shape[0]
    n = n_gx * n_gy
    sizes = (n_gx, n_gy, nx, ny, nz, local_rec, n_rec)
    positions = [r.reshape(n_rec // LANES, LANES) for r in (receiver_x, receiver_y)]
    anywhere = pl.BlockSpec(memory_space=pltpu.HBM)
    block = jax.ShapeDtypeStruct((nx, ny, nz), jnp.float32)
    held = pltpu.VMEM((nx, ny, nz), jnp.float32)
    ends = pl.pallas_call(
        functools.partial(kernel, sizes),
        out_shape=(held,) * 3,
        in_specs=[anywhere] * 16 + [pl.BlockSpec(memory_space=pltpu.SMEM)],
        out_specs=(pl.BlockSpec(memory_space=pltpu.VMEM),) * 3,
        scratch_shapes=[
            *[pltpu.VMEM((2, nx + 2 * DEEP, ny + 2 * TOP, nz), jnp.float32)] * (2 * STEPS + 2),
            *[pltpu.VMEM((2, nx, ny + 8, nz), jnp.float32)] * 2,
            pltpu.VMEM((13, nx + 2 * DEEP, ny + 8, nz), jnp.float32),
            pltpu.VMEM((5, nx, ny, nz), jnp.float32),
            pltpu.VMEM((5, nx + 2 * DEEP, ny + 2 * TOP, nz), jnp.float32),
            pltpu.VMEM((STEPS, nx + 2 * DEEP, ny + 8, nz), jnp.float32),
            pltpu.VMEM((samples, local_rec), jnp.float32),
            pltpu.VMEM((8, LANES), jnp.float32),
            pltpu.VMEM((n * 8, LANES), jnp.float32),
            pltpu.VMEM((2, n_rec // LANES, LANES), jnp.int32),
            pltpu.VMEM(((nx + 2 * DEEP + 7) // 8 * 8, n_rec), jnp.float32),
            pltpu.VMEM((ny + 8, n_rec), jnp.float32),
            pltpu.VMEM((16 * n + 48 * (nx + 4) * (ny + 4), LANES), jnp.float32),
            pltpu.SemaphoreType.DMA((6,)),
            pltpu.SemaphoreType.DMA((2,)),
            pltpu.SemaphoreType.DMA((8,)),
        ],
        compiler_params=pltpu.CompilerParams(
            collective_id=0, has_side_effects=True, vmem_limit_bytes=48 * 1024 * 1024
        ),
        name="window",
    )(*[pltpu.with_memory_space_constraint(a, pltpu.HBM) for a in (*args[:13], traces, *positions)], segment_start)
    return pl.pallas_call(
        write_out,
        out_shape=(block,) * 3,
        in_specs=[pl.BlockSpec(memory_space=pltpu.VMEM)] * 3,
        out_specs=(pl.BlockSpec(memory_space=pltpu.HBM),) * 3,
        scratch_shapes=[pltpu.SemaphoreType.DMA((3,))],
        compiler_params=pltpu.CompilerParams(vmem_limit_bytes=1024 * 1024),
        name="write_out",
    )(*[pltpu.with_memory_space_constraint(end, pltpu.VMEM) for end in ends])


def solution(mesh):
    block, cell = P(("shot", "gx"), "gy", None), P("gx", "gy", None)
    return jax.shard_map(
        per_device,
        mesh=mesh,
        in_specs=(block,) * 8 + (cell,) * 5 + (P("shot", ("gx", "gy")), P(), P(), P()),
        out_specs=(block,) * 3,
        check_vma=False,
    )
```

```python
import functools

import jax
import jax.numpy as jnp
from jax import lax
from jax.experimental import pallas as pl
from jax.experimental.pallas import tpu as pltpu
from jax.sharding import PartitionSpec as P

STEPS = 4
REC_DEPTH = 4
DEEP = 3
RINGS = (0, 2, 1, 0)
BASE = 8
TOP = 12
LANES = 128
SIDES = ((0, -1), (0, 1), (-1, 0), (1, 0), (-1, -1), (-1, 1), (1, -1), (1, 1))
MESH = pl.DeviceIdType.MESH
scope = jax.named_scope


def sine(x):
    s = x * x
    c = 1.6059044e-10
    for k in (-2.5052108e-8, 2.7557319e-6, -1.98412698e-4, 8.3333333e-3, -1.66666667e-1):
        c = c * s + k
    return x + x * (s * c)


def cosine(x):
    s = x * x
    c = -1.1470746e-11
    for k in (2.0876757e-9, -2.7557319e-7, 2.4801587e-5, -1.38888889e-3, 4.16666667e-2, -0.5):
        c = c * s + k
    return 1.0 + s * c


def kernel(sizes, *refs):
    n_gx, n_gy, nx, ny, nz, local_rec, n_rec = sizes
    fields, model = refs[:8], refs[8:13]
    traces, rec_x, rec_y, start = refs[13:17]
    image, p_last, q_last = refs[17:20]
    (*held, old_0, old_1, coef, earth, unit, inject, rows, window, gathered, rec_pos, hot_x, hot_y, pool,
     load_sem, send_sem, recv_sem, ready) = refs[20:]
    waves = (held[:STEPS + 1], held[STEPS + 1:])
    olds = (old_0, old_1)
    wide = ny + 8
    n = n_gx * n_gy
    gx, gy = lax.axis_index("gx"), lax.axis_index("gy")
    me = gx * n_gy + gy

    barrier = pltpu.get_barrier_semaphore()

    def peer_id(i):
        peer = lax.rem(me + n - i, n)
        return {"gx": peer // n_gy, "gy": lax.rem(peer, n_gy)}

    def await_rows(sem, count):
        part = pool.at[pl.ds(0, count)]
        pltpu.make_async_copy(part, part, sem).wait()

    inner_x, inner_y = pl.ds(DEEP, nx), pl.ds(TOP, ny)

    with scope("loads"):
        for g in range(2):
            for f in range(2):
                pltpu.make_async_copy(
                    fields[4 * g + 2 * f + 1], waves[g][0].at[f, inner_x, inner_y], load_sem.at[0]
                ).start()
        for i in range(5):
            pltpu.make_async_copy(model[i], earth.at[i], load_sem.at[1]).start()
        load_traces = pltpu.make_async_copy(traces, rows, load_sem.at[2])
        load_traces.start()

    def there(dx, dy):
        ok = None
        for d, pos, count in ((dx, gx, n_gx), (dy, gy, n_gy)):
            if d:
                test = pos + d < count if d > 0 else pos + d >= 0
                ok = test if ok is None else ok & test
        return ok

    def tell_neighbours(sem):
        for dx, dy in SIDES:
            @pl.when(there(dx, dy))
            def _():
                pl.semaphore_signal(
                    sem, inc=1, device_id={"gx": gx + dx, "gy": gy + dy}, device_id_type=MESH
                )

    def count_beside(pos, count):
        return jnp.where(pos > 0, 1, 0) + jnp.where(pos < count - 1, 1, 0)

    neighbours = (1 + count_beside(gx, n_gx)) * (1 + count_beside(gy, n_gy)) - 1
    rounds = max(n_gx, n_gy) - 2

    def hear_neighbours(sem):
        pl.semaphore_wait(sem, neighbours)

    with scope("greet"):
        tell_neighbours(barrier)

    def span(d, start, size, first, last):
        if d == 0:
            return pl.ds(start, size), pl.ds(start, size)
        if d > 0:
            return pl.ds(start + size - last, last - first), pl.ds(start - last, last - first)
        return pl.ds(start + first, last - first), pl.ds(start + size + first, last - first)

    def send(ref, slot, near, far, corner, out=0):
        for dx, dy in SIDES:
            first, last = (0, corner) if dx and dy else (near, far)
            if last == first:
                continue

            @pl.when(there(dx, dy))
            def _():
                src_x, dst_x = span(dx, DEEP, nx, first, last)
                src_y, dst_y = span(dy, TOP, ny, first, last)
                pltpu.make_async_remote_copy(
                    src_ref=ref.at[:, src_x, src_y],
                    dst_ref=ref.at[:, dst_x, dst_y],
                    send_sem=send_sem.at[out],
                    recv_sem=recv_sem.at[slot],
                    device_id={"gx": gx + dx, "gy": gy + dy},
                    device_id_type=MESH,
                ).start()

    def halo_rows(count, layers, corner, beside_x, beside_y):
        faces = beside_x * ny + beside_y * nx
        return count * (layers * faces + beside_x * beside_y * corner * corner)

    def by_place(act):
        for beside_x in range(min(n_gx, 3)):
            for beside_y in range(min(n_gy, 3)):
                here_x = jnp.where(gx > 0, 1, 0) + jnp.where(gx < n_gx - 1, 1, 0) == beside_x
                here_y = jnp.where(gy > 0, 1, 0) + jnp.where(gy < n_gy - 1, 1, 0) == beside_y

                @pl.when(here_x & here_y)
                def _():
                    act(beside_x, beside_y)

    def await_halo(slot, *groups, sems=recv_sem):
        def act(beside_x, beside_y):
            total = sum(halo_rows(*group, beside_x, beside_y) for group in groups)
            if total:
                await_rows(sems.at[slot], total)

        by_place(act)

    with scope("wait_now"):
        await_rows(load_sem.at[0], 4 * nx * ny)
    with scope("barrier"):
        hear_neighbours(barrier)
    with scope("send_src0"):
        if rounds > 0:
            tell_neighbours(ready.at[0])
        send(waves[0][0], 0, 0, 1, 2)

    with scope("wait_model"):
        await_rows(load_sem.at[1], 5 * nx * ny)

    def units(x, carry):
        v = earth[0, x]
        f_e = 1.0 + 2.0 * earth[1, x]
        f_d = jnp.sqrt(1.0 + 2.0 * earth[2, x])
        tilt = earth[3, x]
        half = 0.5 * earth[4, x]
        sin_t = sine(tilt)
        sin_h, cos_h = sine(half), cosine(half)
        sin_a = 2.0 * sin_h * cos_h
        cos_a = 1.0 - 2.0 * sin_h * sin_h
        to = (x + DEEP, inner_y)
        unit[(0, *to)] = v
        unit[(1, *to)] = v * f_e
        unit[(2, *to)] = v * f_d
        unit[(3, *to)] = sin_t * cos_a
        unit[(4, *to)] = sin_t * sin_a
        return carry

    with scope("units"):
        lax.fori_loop(0, nx, units, 0, unroll=nx)
    with scope("send_rec0"):
        send(waves[1][0], 1, 0, 1, 2)

    per_row = LANES // local_rec
    packed = STEPS // per_row
    with scope("window"):
        load_traces.wait()
        window[...] = jnp.zeros_like(window)
        window[0:STEPS, 0:local_rec] = rows[pl.ds(start[0], STEPS), :]
        sample = window[...]
        for r in range(packed):
            row = sample[r * per_row:r * per_row + 1]
            for j in range(1, per_row):
                row = row + pltpu.roll(sample[r * per_row + j:r * per_row + j + 1], j * local_rec, 1)
            window[r:r + 1] = row
        mine = pl.ds(pl.multiple_of(me * 8, 8), packed)
        gathered[mine] = window[0:packed]

    def far_start(i, carry):
        pltpu.make_async_remote_copy(
            src_ref=window.at[0:packed],
            dst_ref=gathered.at[mine],
            send_sem=send_sem.at[0],
            recv_sem=recv_sem.at[7],
            device_id=peer_id(i),
            device_id_type=MESH,
        ).start()
        return carry

    with scope("send_model"):
        send(unit, 2, 0, 2, 2)
    with scope("send_layer"):
        send(waves[0][0], 3, 1, 2, 0)
        send(waves[1][0], 3, 1, 2, 0)
    for g in range(2):
        for f in range(2):
            pltpu.make_async_copy(
                fields[4 * g + 2 * f], olds[g].at[f, :, pl.ds(TOP - BASE, ny)], load_sem.at[3]
            ).start()
    load_x = pltpu.make_async_copy(rec_x, rec_pos.at[0], load_sem.at[4])
    load_y = pltpu.make_async_copy(rec_y, rec_pos.at[1], load_sem.at[5])
    load_x.start()
    load_y.start()

    with scope("round"):
        if rounds > 0:
            hear_neighbours(ready.at[0])
        if rounds > 1:
            tell_neighbours(ready.at[1])

    def clear(ref, count, depth):
        zeros = jnp.zeros((wide, nz), jnp.float32)
        for edge, first in ((gx == 0, DEEP - depth), (gx == n_gx - 1, DEEP + nx)):
            @pl.when(edge)
            def _():
                for f in range(count):
                    for x in range(first, first + depth):
                        ref[f, x, BASE:BASE + wide] = zeros
        for edge, first in ((gy == 0, TOP - depth), (gy == n_gy - 1, TOP + ny)):
            @pl.when(edge)
            def _():
                for f in range(count):
                    ref[f, :, first:first + depth] = jnp.zeros((nx + 2 * DEEP, depth, nz), jnp.float32)

    with scope("clear"):
        for g in range(2):
            clear(waves[g][0], 2, 2)
            clear(waves[g][1], 2, 3)
        clear(unit, 5, 2)

    def after(value):
        return pltpu.roll(value, nz - 1, 1)

    def before(value):
        return pltpu.roll(value, 1, 1)

    def factors(x, first, count):
        lane = lax.broadcasted_iota(jnp.int32, (count, nz), 1)
        at = pl.ds(first, count)
        to = pl.ds(first - BASE, count)
        n_x, n_y = unit[3, x, at], unit[4, x, at]
        a_xx, a_yy = n_x * n_x, n_y * n_y
        a_zz = 1.0 - (a_xx + a_yy)
        half_z = 0.5 * jnp.sqrt(a_zz)
        a_xz, a_yz = half_z * n_x, half_z * n_y
        coef[0, x, to] = a_xx
        coef[1, x, to] = a_yy
        coef[4, x, to] = 1.0 - a_xx
        coef[5, x, to] = 1.0 - a_yy
        coef[8, x, to] = (0.5 * n_x) * n_y
        for shift, edge, i in ((before, lane == 0, 0), (after, lane == nz - 1, 1)):
            moved = shift(a_zz)
            coef[2 + i, x, to] = jnp.where(edge, 0.0, moved)
            coef[6 + i, x, to] = jnp.where(edge, 0.0, 1.0 - moved)
            coef[9 + 2 * i, x, to] = jnp.where(edge, 0.0, shift(a_xz))
            coef[10 + 2 * i, x, to] = jnp.where(edge, 0.0, shift(a_yz))

    def inner_factors(x, carry):
        factors(x, TOP, ny)
        return carry

    def outer_factors(x, carry):
        factors(x, BASE, 8)
        factors(x, BASE + wide - 8, 8)
        return carry

    with scope("inner_factors"):
        lax.fori_loop(DEEP, DEEP + nx, inner_factors, 0, unroll=nx)

    def rotated(now, f, x, lo, count, center, weights):
        sign, w_x, w_y, w_up, w_down = weights
        mid, up, down = pl.ds(lo, count), pl.ds(lo + 1, count), pl.ds(lo - 1, count)
        at = pl.ds(lo - BASE, count)
        x_up, x_down = now[f, x + 1, mid], now[f, x - 1, mid]
        y_up, y_down = now[f, x, up], now[f, x, down]
        d_x, d_y = x_up - x_down, y_up - y_down
        d_xy = (now[f, x + 1, up] - now[f, x + 1, down]) - (now[f, x - 1, up] - now[f, x - 1, down])
        flat = coef[w_x, x, at] * (x_up + x_down) + coef[w_y, x, at] * (y_up + y_down)
        mixed = coef[8, x, at] * d_xy
        above, below = coef[w_up, x, at] * center, coef[w_down, x, at] * center
        mixed_above = coef[9, x, at] * d_x + coef[10, x, at] * d_y
        mixed_below = coef[11, x, at] * d_x + coef[12, x, at] * d_y
        if sign > 0:
            return (flat + mixed) + (after(above + mixed_above) + before(below - mixed_below))
        return (flat - mixed) + (after(above - mixed_above) + before(below + mixed_below))

    def step(g, level):
        now = waves[g][level]
        ring = RINGS[level]
        lo, count = (BASE, wide) if ring else (TOP, ny)
        mid = pl.ds(lo, count)

        def plane(x, carry):
            p_now, q_now = now[0, x, mid], now[1, x, mid]
            p_two, q_two = p_now + p_now, q_now + q_now
            across = rotated(now, 0, x, lo, count, p_now, (-1, 4, 5, 6, 7)) - (p_two + p_two)
            q_axis = rotated(now, 1, x, lo, count, q_now, (1, 0, 1, 2, 3)) - q_two
            v_d = unit[2, x, mid]
            if level:
                p_prev, q_prev = waves[g][level - 1][0, x, mid], waves[g][level - 1][1, x, mid]
            else:
                p_prev, q_prev = olds[g][0, x - DEEP, TOP - BASE:TOP - BASE + ny], olds[g][1, x - DEEP, TOP - BASE:TOP - BASE + ny]
            p_next = (p_two - p_prev) + (unit[1, x, mid] * across + v_d * q_axis)
            if g == 1 and level:
                p_next = p_next + inject[STEPS - 1 - level, x, pl.ds(lo - BASE, count)]
            if g == 0 and level == STEPS - 1:
                waves[g][level + 1][0, x, mid] = p_next
                return carry
            q_next = (q_two - q_prev) + (v_d * across + unit[0, x, mid] * q_axis)
            if g == 1 and level == STEPS - 1:
                p_last[x - DEEP] = p_next
                q_last[x - DEEP] = q_next
                total = waves[0][0][0, x, mid] * p_next
                for k in range(STEPS):
                    total = total + waves[1][k][0, x, mid] * waves[0][STEPS - k][0, x, mid]
                image[x - DEEP] = total
            else:
                waves[g][level + 1][0, x, mid] = p_next
                waves[g][level + 1][1, x, mid] = q_next
            return carry

        lax.fori_loop(DEEP - ring, DEEP + nx + ring, plane, 0, unroll=nx + 2 * ring)

    n_rows = n_rec // LANES
    wide_x = hot_x.shape[0]

    def find(i, carry):
        to = pl.ds(pl.multiple_of(i * LANES, LANES), LANES)
        x_id = lax.broadcasted_iota(jnp.int32, (wide_x, LANES), 0) + (gx * nx - DEEP)
        y_id = lax.broadcasted_iota(jnp.int32, (wide, LANES), 0) + (gy * ny - (TOP - BASE))
        hot_x[:, to] = jnp.where(rec_pos[0, pl.ds(i, 1)] == x_id, 1.0, 0.0)
        hot_y[:, to] = jnp.where(rec_pos[1, pl.ds(i, 1)] == y_id, 1.0, 0.0)
        return carry

    with scope("find"):
        load_x.wait()
        load_y.wait()
        lax.fori_loop(0, n_rows, find, 0, unroll=8)

    def make_planes():
        segment = lax.broadcasted_iota(jnp.int32, (n_rows, LANES), 1) // local_rec
        parts = []
        for k in range(STEPS):
            r, own = k // per_row, k % per_row
            sample = None
            for j in range(per_row):
                piece = gathered[pl.ds(j * 8 + r, n_rows, stride=per_row * 8), :]
                piece = jnp.where(segment == own, piece, 0.0)
                if j != own:
                    piece = pltpu.roll(piece, (j - own) * local_rec % LANES, 1)
                sample = piece if sample is None else sample + piece
            for _ in range(3):
                part = sample.astype(jnp.bfloat16).astype(jnp.float32)
                parts.append(part)
                sample = sample - part
        chunk = min(8, n_rows)
        total = jnp.zeros((3 * STEPS * wide, wide_x), jnp.float32)
        for base in range(0, n_rows, chunk):
            columns = slice(base * LANES, (base + chunk) * LANES)
            left = jnp.concatenate(
                [
                    jnp.concatenate(
                        [hot_y[:, i * LANES:(i + 1) * LANES] * part[i:i + 1] for part in parts], axis=0
                    )
                    for i in range(base, base + chunk)
                ],
                axis=1,
            )
            total = total + lax.dot_general(
                left, hot_x[:, columns], (((1,), (1,)), ((), ())), preferred_element_type=jnp.float32
            )
        here = lax.broadcasted_iota(jnp.int32, (wide, nz), 1) == REC_DEPTH
        for k in range(STEPS):
            three = [total[(3 * k + i) * wide:(3 * k + i + 1) * wide] for i in range(3)]
            plane = (three[0] + three[1]) + three[2]
            for x in range(nx + 2 * DEEP):
                inject[k, x] = jnp.where(here, plane[:, x:x + 1], 0.0)

    with scope("rounds"):
        for i in range(1, rounds):
            hear_neighbours(ready.at[i])
            if i + 1 < rounds:
                tell_neighbours(ready.at[i + 1])
    with scope("far_start"):
        lax.fori_loop(1, n, far_start, 0, unroll=min(15, n - 1))

    with scope("wait_prev"):
        await_rows(load_sem.at[3], 4 * nx * ny)
    with scope("wait_src0"):
        await_halo(0, (2, 1, 2))
    with scope("src_step0"):
        step(0, 0)
    with scope("send_src1"):
        send(waves[0][1], 5, 0, 3, 3)
    with scope("wait_rec0"):
        await_halo(1, (2, 1, 2))
    with scope("rec_step0"):
        step(1, 0)
    with scope("send_rec1"):
        send(waves[1][1], 6, 0, 3, 3, out=1)
    with scope("wait_model_halo"):
        await_halo(2, (5, 2, 2))
    with scope("outer_factors"):
        lax.fori_loop(DEEP, DEEP + nx, outer_factors, 0, unroll=nx)
        for x in (DEEP - 2, DEEP - 1, DEEP + nx, DEEP + nx + 1):
            factors(x, BASE, wide)
    with scope("wait_src1"):
        await_halo(3, (4, 1, 0))
        await_halo(5, (2, 3, 3))
    for level in range(1, STEPS):
        with scope("src_step%d" % level):
            step(0, level)
    with scope("wait_far"):
        if n > 1:
            await_rows(recv_sem.at[7], packed * (n - 1))
    with scope("planes"):
        make_planes()
    with scope("wait_rec1"):
        await_halo(6, (2, 3, 3))
        await_halo(1, (2, 3, 3), sems=send_sem)

    def add_samples(x, carry):
        ext = pl.ds(BASE, wide)
        waves[1][1][0, x, ext] = waves[1][1][0, x, ext] + inject[STEPS - 1, x]
        return carry

    with scope("add_samples"):
        lax.fori_loop(0, nx + 2 * DEEP, add_samples, 0, unroll=nx + 2 * DEEP)
    for level in range(1, STEPS):
        with scope("rec_step%d" % level):
            step(1, level)

    def finish(beside_x, beside_y):
        total = packed * (n - 1)
        for group in ((4, 1, 2), (5, 2, 2), (4, 1, 0), (2, 3, 3)):
            total += halo_rows(*group, beside_x, beside_y)
        if total:
            await_rows(send_sem.at[0], total)

    with scope("finish"):
        by_place(finish)


def write_out(*refs):
    values, results, done = refs[:3], refs[3:6], refs[6]
    copies = [pltpu.make_async_copy(values[i], results[i], done.at[i]) for i in range(3)]
    for copy in copies:
        copy.start()
    for copy in copies:
        copy.wait()


def per_device(*args):
    nx, ny, nz = args[0].shape
    n_gx, n_gy = lax.axis_size("gx"), lax.axis_size("gy")
    traces, receiver_x, receiver_y, segment_start = args[13:]
    samples, local_rec = traces.shape
    n_rec = receiver_x.shape[0]
    n = n_gx * n_gy
    sizes = (n_gx, n_gy, nx, ny, nz, local_rec, n_rec)
    positions = [r.reshape(n_rec // LANES, LANES) for r in (receiver_x, receiver_y)]
    anywhere = pl.BlockSpec(memory_space=pltpu.HBM)
    block = jax.ShapeDtypeStruct((nx, ny, nz), jnp.float32)
    held = pltpu.VMEM((nx, ny, nz), jnp.float32)
    ends = pl.pallas_call(
        functools.partial(kernel, sizes),
        out_shape=(held,) * 3,
        in_specs=[anywhere] * 16 + [pl.BlockSpec(memory_space=pltpu.SMEM)],
        out_specs=(pl.BlockSpec(memory_space=pltpu.VMEM),) * 3,
        scratch_shapes=[
            *[pltpu.VMEM((2, nx + 2 * DEEP, ny + 2 * TOP, nz), jnp.float32)] * (2 * STEPS + 2),
            *[pltpu.VMEM((2, nx, ny + 8, nz), jnp.float32)] * 2,
            pltpu.VMEM((13, nx + 2 * DEEP, ny + 8, nz), jnp.float32),
            pltpu.VMEM((5, nx, ny, nz), jnp.float32),
            pltpu.VMEM((5, nx + 2 * DEEP, ny + 2 * TOP, nz), jnp.float32),
            pltpu.VMEM((STEPS, nx + 2 * DEEP, ny + 8, nz), jnp.float32),
            pltpu.VMEM((samples, local_rec), jnp.float32),
            pltpu.VMEM((8, LANES), jnp.float32),
            pltpu.VMEM((n * 8, LANES), jnp.float32),
            pltpu.VMEM((2, n_rec // LANES, LANES), jnp.int32),
            pltpu.VMEM(((nx + 2 * DEEP + 7) // 8 * 8, n_rec), jnp.float32),
            pltpu.VMEM((ny + 8, n_rec), jnp.float32),
            pltpu.VMEM((16 * n + 48 * (nx + 4) * (ny + 4), LANES), jnp.float32),
            pltpu.SemaphoreType.DMA((6,)),
            pltpu.SemaphoreType.DMA((2,)),
            pltpu.SemaphoreType.DMA((8,)),
            pltpu.SemaphoreType.REGULAR((max(n_gx, n_gy, 3) - 2,)),
        ],
        compiler_params=pltpu.CompilerParams(
            collective_id=0, has_side_effects=True, vmem_limit_bytes=48 * 1024 * 1024
        ),
        name="window",
    )(*[pltpu.with_memory_space_constraint(a, pltpu.HBM) for a in (*args[:13], traces, *positions)], segment_start)
    return pl.pallas_call(
        write_out,
        out_shape=(block,) * 3,
        in_specs=[pl.BlockSpec(memory_space=pltpu.VMEM)] * 3,
        out_specs=(pl.BlockSpec(memory_space=pltpu.HBM),) * 3,
        scratch_shapes=[pltpu.SemaphoreType.DMA((3,))],
        compiler_params=pltpu.CompilerParams(vmem_limit_bytes=1024 * 1024),
        name="write_out",
    )(*[pltpu.with_memory_space_constraint(end, pltpu.VMEM) for end in ends])


def solution(mesh):
    block, cell = P(("shot", "gx"), "gy", None), P("gx", "gy", None)
    return jax.shard_map(
        per_device,
        mesh=mesh,
        in_specs=(block,) * 8 + (cell,) * 5 + (P("shot", ("gx", "gy")), P(), P(), P()),
        out_specs=(block,) * 3,
        check_vma=False,
    )
```

```python
import functools

import jax
import jax.numpy as jnp
from jax import lax
from jax.experimental import pallas as pl
from jax.experimental.pallas import tpu as pltpu
from jax.sharding import PartitionSpec as P

STEPS = 4
REC_DEPTH = 4
DEEP = 3
RINGS = (0, 2, 1, 0)
BASE = 8
TOP = 12
LANES = 128
SIDES = ((0, -1), (0, 1), (-1, 0), (1, 0), (-1, -1), (-1, 1), (1, -1), (1, 1))
MESH = pl.DeviceIdType.MESH
scope = jax.named_scope


def sine(x):
    s = x * x
    c = 1.6059044e-10
    for k in (-2.5052108e-8, 2.7557319e-6, -1.98412698e-4, 8.3333333e-3, -1.66666667e-1):
        c = c * s + k
    return x + x * (s * c)


def cosine(x):
    s = x * x
    c = -1.1470746e-11
    for k in (2.0876757e-9, -2.7557319e-7, 2.4801587e-5, -1.38888889e-3, 4.16666667e-2, -0.5):
        c = c * s + k
    return 1.0 + s * c


def kernel(sizes, *refs):
    n_gx, n_gy, nx, ny, nz, local_rec, n_rec = sizes
    fields, model = refs[:8], refs[8:13]
    traces, rec_x, rec_y, start = refs[13:17]
    image, p_last, q_last = refs[17:20]
    (*held, old_0, old_1, coef, earth, unit, inject, rows, window, gathered, rec_pos, hot_x, hot_y, pool,
     load_sem, send_sem, recv_sem, ready) = refs[20:]
    waves = (held[:STEPS + 1], held[STEPS + 1:])
    olds = (old_0, old_1)
    wide = ny + 8
    n = n_gx * n_gy
    gx, gy = lax.axis_index("gx"), lax.axis_index("gy")
    me = gx * n_gy + gy

    barrier = pltpu.get_barrier_semaphore()

    def peer_id(i):
        peer = lax.rem(me + n - i, n)
        return {"gx": peer // n_gy, "gy": lax.rem(peer, n_gy)}

    def await_rows(sem, count):
        part = pool.at[pl.ds(0, count)]
        pltpu.make_async_copy(part, part, sem).wait()

    inner_x, inner_y = pl.ds(DEEP, nx), pl.ds(TOP, ny)

    with scope("loads"):
        for g in range(2):
            for f in range(2):
                pltpu.make_async_copy(
                    fields[4 * g + 2 * f + 1], waves[g][0].at[f, inner_x, inner_y], load_sem.at[0]
                ).start()
        for i in range(5):
            pltpu.make_async_copy(model[i], earth.at[i], load_sem.at[1]).start()
        load_traces = pltpu.make_async_copy(traces, rows, load_sem.at[2])
        load_traces.start()

    def there(dx, dy):
        ok = None
        for d, pos, count in ((dx, gx, n_gx), (dy, gy, n_gy)):
            if d:
                test = pos + d < count if d > 0 else pos + d >= 0
                ok = test if ok is None else ok & test
        return ok

    def tell_neighbours(sem):
        for dx, dy in SIDES:
            @pl.when(there(dx, dy))
            def _():
                pl.semaphore_signal(
                    sem, inc=1, device_id={"gx": gx + dx, "gy": gy + dy}, device_id_type=MESH
                )

    def count_beside(pos, count):
        return jnp.where(pos > 0, 1, 0) + jnp.where(pos < count - 1, 1, 0)

    neighbours = (1 + count_beside(gx, n_gx)) * (1 + count_beside(gy, n_gy)) - 1
    rounds = max(n_gx, n_gy) - 2

    def hear_neighbours(sem):
        pl.semaphore_wait(sem, neighbours)

    with scope("greet"):
        tell_neighbours(barrier)

    def span(d, start, size, first, last):
        if d == 0:
            return pl.ds(start, size), pl.ds(start, size)
        if d > 0:
            return pl.ds(start + size - last, last - first), pl.ds(start - last, last - first)
        return pl.ds(start + first, last - first), pl.ds(start + size + first, last - first)

    def send(ref, slot, near, far, corner, out=0):
        for dx, dy in SIDES:
            first, last = (0, corner) if dx and dy else (near, far)
            if last == first:
                continue

            @pl.when(there(dx, dy))
            def _():
                src_x, dst_x = span(dx, DEEP, nx, first, last)
                src_y, dst_y = span(dy, TOP, ny, first, last)
                pltpu.make_async_remote_copy(
                    src_ref=ref.at[:, src_x, src_y],
                    dst_ref=ref.at[:, dst_x, dst_y],
                    send_sem=send_sem.at[out],
                    recv_sem=recv_sem.at[slot],
                    device_id={"gx": gx + dx, "gy": gy + dy},
                    device_id_type=MESH,
                ).start()

    def halo_rows(count, layers, corner, beside_x, beside_y):
        faces = beside_x * ny + beside_y * nx
        return count * (layers * faces + beside_x * beside_y * corner * corner)

    def by_place(act):
        for beside_x in range(min(n_gx, 3)):
            for beside_y in range(min(n_gy, 3)):
                here_x = jnp.where(gx > 0, 1, 0) + jnp.where(gx < n_gx - 1, 1, 0) == beside_x
                here_y = jnp.where(gy > 0, 1, 0) + jnp.where(gy < n_gy - 1, 1, 0) == beside_y

                @pl.when(here_x & here_y)
                def _():
                    act(beside_x, beside_y)

    def await_halo(slot, *groups, sems=recv_sem):
        def act(beside_x, beside_y):
            total = sum(halo_rows(*group, beside_x, beside_y) for group in groups)
            if total:
                await_rows(sems.at[slot], total)

        by_place(act)

    with scope("wait_now"):
        await_rows(load_sem.at[0], 4 * nx * ny)
    with scope("barrier"):
        hear_neighbours(barrier)
    with scope("send_src0"):
        if rounds > 0:
            tell_neighbours(ready.at[0])
        send(waves[0][0], 0, 0, 1, 2)

    with scope("wait_model"):
        await_rows(load_sem.at[1], 5 * nx * ny)

    def units(x, carry):
        v = earth[0, x]
        f_e = 1.0 + 2.0 * earth[1, x]
        f_d = jnp.sqrt(1.0 + 2.0 * earth[2, x])
        tilt = earth[3, x]
        half = 0.5 * earth[4, x]
        sin_t = sine(tilt)
        sin_h, cos_h = sine(half), cosine(half)
        sin_a = 2.0 * sin_h * cos_h
        cos_a = 1.0 - 2.0 * sin_h * sin_h
        to = (x + DEEP, inner_y)
        unit[(0, *to)] = v
        unit[(1, *to)] = v * f_e
        unit[(2, *to)] = v * f_d
        unit[(3, *to)] = sin_t * cos_a
        unit[(4, *to)] = sin_t * sin_a
        return carry

    with scope("units"):
        lax.fori_loop(0, nx, units, 0, unroll=nx)
    with scope("send_rec0"):
        send(waves[1][0], 1, 0, 1, 2)

    per_row = LANES // local_rec
    packed = STEPS // per_row
    with scope("window"):
        load_traces.wait()
        window[...] = jnp.zeros_like(window)
        window[0:STEPS, 0:local_rec] = rows[pl.ds(start[0], STEPS), :]
        sample = window[...]
        for r in range(packed):
            row = sample[r * per_row:r * per_row + 1]
            for j in range(1, per_row):
                row = row + pltpu.roll(sample[r * per_row + j:r * per_row + j + 1], j * local_rec, 1)
            window[r:r + 1] = row
        mine = pl.ds(pl.multiple_of(me * 8, 8), packed)
        gathered[mine] = window[0:packed]

    def far_start(i, carry):
        pltpu.make_async_remote_copy(
            src_ref=window.at[0:packed],
            dst_ref=gathered.at[mine],
            send_sem=send_sem.at[0],
            recv_sem=recv_sem.at[7],
            device_id=peer_id(i),
            device_id_type=MESH,
        ).start()
        return carry

    with scope("send_model"):
        send(unit, 2, 0, 2, 2)
    with scope("send_layer"):
        send(waves[0][0], 3, 1, 2, 0)
        send(waves[1][0], 3, 1, 2, 0)
    for g in range(2):
        for f in range(2):
            pltpu.make_async_copy(
                fields[4 * g + 2 * f], olds[g].at[f, :, pl.ds(TOP - BASE, ny)], load_sem.at[3]
            ).start()
    load_x = pltpu.make_async_copy(rec_x, rec_pos.at[0], load_sem.at[4])
    load_y = pltpu.make_async_copy(rec_y, rec_pos.at[1], load_sem.at[5])
    load_x.start()
    load_y.start()

    with scope("round"):
        if rounds > 0:
            hear_neighbours(ready.at[0])
        if rounds > 1:
            tell_neighbours(ready.at[1])

    def clear(ref, count, depth):
        zeros = jnp.zeros((wide, nz), jnp.float32)
        for edge, first in ((gx == 0, DEEP - depth), (gx == n_gx - 1, DEEP + nx)):
            @pl.when(edge)
            def _():
                for f in range(count):
                    for x in range(first, first + depth):
                        ref[f, x, BASE:BASE + wide] = zeros
        for edge, first in ((gy == 0, TOP - depth), (gy == n_gy - 1, TOP + ny)):
            @pl.when(edge)
            def _():
                for f in range(count):
                    ref[f, :, first:first + depth] = jnp.zeros((nx + 2 * DEEP, depth, nz), jnp.float32)

    with scope("clear"):
        for g in range(2):
            clear(waves[g][0], 2, 2)
            clear(waves[g][1], 2, 3)
        clear(unit, 5, 2)

    def after(value):
        return pltpu.roll(value, nz - 1, 1)

    def before(value):
        return pltpu.roll(value, 1, 1)

    def factors(x, first, count):
        lane = lax.broadcasted_iota(jnp.int32, (count, nz), 1)
        at = pl.ds(first, count)
        to = pl.ds(first - BASE, count)
        n_x, n_y = unit[3, x, at], unit[4, x, at]
        a_xx, a_yy = n_x * n_x, n_y * n_y
        a_zz = 1.0 - (a_xx + a_yy)
        half_z = 0.5 * jnp.sqrt(a_zz)
        a_xz, a_yz = half_z * n_x, half_z * n_y
        coef[0, x, to] = a_xx
        coef[1, x, to] = a_yy
        coef[4, x, to] = 1.0 - a_xx
        coef[5, x, to] = 1.0 - a_yy
        coef[8, x, to] = (0.5 * n_x) * n_y
        for shift, edge, i in ((before, lane == 0, 0), (after, lane == nz - 1, 1)):
            moved = shift(a_zz)
            coef[2 + i, x, to] = jnp.where(edge, 0.0, moved)
            coef[6 + i, x, to] = jnp.where(edge, 0.0, 1.0 - moved)
            coef[9 + 2 * i, x, to] = jnp.where(edge, 0.0, shift(a_xz))
            coef[10 + 2 * i, x, to] = jnp.where(edge, 0.0, shift(a_yz))

    def inner_factors(x, carry):
        factors(x, TOP, ny)
        return carry

    def outer_factors(x, carry):
        factors(x, BASE, 8)
        factors(x, BASE + wide - 8, 8)
        return carry

    with scope("inner_factors"):
        lax.fori_loop(DEEP, DEEP + nx, inner_factors, 0, unroll=nx)

    def rotated(now, f, x, lo, count, center, weights):
        sign, w_x, w_y, w_up, w_down = weights
        mid, up, down = pl.ds(lo, count), pl.ds(lo + 1, count), pl.ds(lo - 1, count)
        at = pl.ds(lo - BASE, count)
        x_up, x_down = now[f, x + 1, mid], now[f, x - 1, mid]
        y_up, y_down = now[f, x, up], now[f, x, down]
        d_x, d_y = x_up - x_down, y_up - y_down
        d_xy = (now[f, x + 1, up] - now[f, x + 1, down]) - (now[f, x - 1, up] - now[f, x - 1, down])
        flat = coef[w_x, x, at] * (x_up + x_down) + coef[w_y, x, at] * (y_up + y_down)
        mixed = coef[8, x, at] * d_xy
        above, below = coef[w_up, x, at] * center, coef[w_down, x, at] * center
        mixed_above = coef[9, x, at] * d_x + coef[10, x, at] * d_y
        mixed_below = coef[11, x, at] * d_x + coef[12, x, at] * d_y
        if sign > 0:
            return (flat + mixed) + (after(above + mixed_above) + before(below - mixed_below))
        return (flat - mixed) + (after(above - mixed_above) + before(below + mixed_below))

    def step(g, level, part=None):
        ring = RINGS[level]
        first, last = DEEP - ring, DEEP + nx + ring
        if part is None:
            plane_range(g, level, first, last, BASE if ring else TOP, wide if ring else ny)
            return
        lo, count, margin = (TOP + 1, ny - 2, 1) if level == 1 else (TOP + 4, ny - 8, 2)
        if part == "inner":
            plane_range(g, level, DEEP + margin, DEEP + nx - margin, lo, count)
        else:
            for edge in ((first, DEEP + margin), (DEEP + nx - margin, last)):
                plane_range(g, level, *edge, BASE, wide)
            for start in (BASE, BASE + wide - 8):
                plane_range(g, level, DEEP + margin, DEEP + nx - margin, start, 8)

    def plane_range(g, level, first, last, lo, count):
        now = waves[g][level]
        mid = pl.ds(lo, count)

        def plane(x, carry):
            p_now, q_now = now[0, x, mid], now[1, x, mid]
            p_two, q_two = p_now + p_now, q_now + q_now
            across = rotated(now, 0, x, lo, count, p_now, (-1, 4, 5, 6, 7)) - (p_two + p_two)
            q_axis = rotated(now, 1, x, lo, count, q_now, (1, 0, 1, 2, 3)) - q_two
            v_d = unit[2, x, mid]
            if level:
                p_prev, q_prev = waves[g][level - 1][0, x, mid], waves[g][level - 1][1, x, mid]
            else:
                p_prev, q_prev = olds[g][0, x - DEEP, TOP - BASE:TOP - BASE + ny], olds[g][1, x - DEEP, TOP - BASE:TOP - BASE + ny]
            p_next = (p_two - p_prev) + (unit[1, x, mid] * across + v_d * q_axis)
            if g == 1 and level:
                p_next = p_next + samples_at(STEPS - 1 - level, x, lo - BASE, count)
            if g == 0 and level == STEPS - 1:
                waves[g][level + 1][0, x, mid] = p_next
                return carry
            q_next = (q_two - q_prev) + (v_d * across + unit[0, x, mid] * q_axis)
            if g == 1 and level == STEPS - 1:
                p_last[x - DEEP] = p_next
                q_last[x - DEEP] = q_next
                total = waves[0][0][0, x, mid] * p_next
                for k in range(STEPS):
                    total = total + waves[1][k][0, x, mid] * waves[0][STEPS - k][0, x, mid]
                image[x - DEEP] = total
            else:
                waves[g][level + 1][0, x, mid] = p_next
                waves[g][level + 1][1, x, mid] = q_next
            return carry

        lax.fori_loop(first, last, plane, 0, unroll=last - first)

    n_rows = n_rec // LANES
    wide_x = hot_x.shape[0]

    def find(i, carry):
        to = pl.ds(pl.multiple_of(i * LANES, LANES), LANES)
        x_id = lax.broadcasted_iota(jnp.int32, (wide_x, LANES), 0) + (gx * nx - DEEP)
        y_id = lax.broadcasted_iota(jnp.int32, (wide, LANES), 0) + (gy * ny - (TOP - BASE))
        hot_x[:, to] = jnp.where(rec_pos[0, pl.ds(i, 1)] == x_id, 1.0, 0.0)
        hot_y[:, to] = jnp.where(rec_pos[1, pl.ds(i, 1)] == y_id, 1.0, 0.0)
        return carry

    with scope("find"):
        load_x.wait()
        load_y.wait()
        lax.fori_loop(0, n_rows, find, 0, unroll=8)

    def make_planes():
        segment = lax.broadcasted_iota(jnp.int32, (n_rows, LANES), 1) // local_rec
        parts = []
        for k in range(STEPS):
            r, own = k // per_row, k % per_row
            sample = None
            for j in range(per_row):
                piece = gathered[pl.ds(j * 8 + r, n_rows, stride=per_row * 8), :]
                piece = jnp.where(segment == own, piece, 0.0)
                if j != own:
                    piece = pltpu.roll(piece, (j - own) * local_rec % LANES, 1)
                sample = piece if sample is None else sample + piece
            for _ in range(3):
                part = sample.astype(jnp.bfloat16).astype(jnp.float32)
                parts.append(part)
                sample = sample - part
        chunk = min(8, n_rows)
        total = jnp.zeros((3 * STEPS * wide, wide_x), jnp.float32)
        for base in range(0, n_rows, chunk):
            columns = slice(base * LANES, (base + chunk) * LANES)
            left = jnp.concatenate(
                [
                    jnp.concatenate(
                        [hot_y[:, i * LANES:(i + 1) * LANES] * part[i:i + 1] for part in parts], axis=0
                    )
                    for i in range(base, base + chunk)
                ],
                axis=1,
            )
            total = total + lax.dot_general(
                left, hot_x[:, columns], (((1,), (1,)), ((), ())), preferred_element_type=jnp.float32
            )
        for k in range(STEPS):
            three = [total[(3 * k + i) * wide:(3 * k + i + 1) * wide] for i in range(3)]
            inject[k] = (three[0] + three[1]) + three[2]

    def samples_at(k, x, first, count):
        lane = lax.broadcasted_iota(jnp.int32, (count, LANES), 1)
        column = pltpu.roll(inject[k, pl.ds(first, count)], lax.rem(LANES + REC_DEPTH - x, LANES), 1)
        return jnp.where(lane == REC_DEPTH, column, 0.0)

    with scope("rounds"):
        for i in range(1, rounds):
            hear_neighbours(ready.at[i])
            if i + 1 < rounds:
                tell_neighbours(ready.at[i + 1])
    with scope("far_start"):
        lax.fori_loop(1, n, far_start, 0, unroll=min(15, n - 1))

    with scope("wait_prev"):
        await_rows(load_sem.at[3], 4 * nx * ny)
    with scope("wait_src0"):
        await_halo(0, (2, 1, 2))
    with scope("src_step0"):
        step(0, 0)
    with scope("send_src1"):
        send(waves[0][1], 5, 0, 3, 3)
    with scope("wait_rec0"):
        await_halo(1, (2, 1, 2))
    with scope("rec_step0"):
        step(1, 0)
    with scope("send_rec1"):
        send(waves[1][1], 6, 0, 3, 3, out=1)
    with scope("wait_model_halo"):
        await_halo(2, (5, 2, 2))
    with scope("outer_factors"):
        lax.fori_loop(DEEP, DEEP + nx, outer_factors, 0, unroll=nx)
        for x in (DEEP - 2, DEEP - 1, DEEP + nx, DEEP + nx + 1):
            factors(x, BASE, wide)
    with scope("src_inner"):
        for level in (1, 2):
            step(0, level, "inner")
    with scope("wait_src1"):
        await_halo(3, (4, 1, 0))
        await_halo(5, (2, 3, 3))
    for level in range(1, STEPS):
        with scope("src_step%d" % level):
            step(0, level, "outer" if level < STEPS - 1 else None)
    with scope("wait_far"):
        if n > 1:
            await_rows(recv_sem.at[7], packed * (n - 1))
    with scope("planes"):
        make_planes()
    with scope("wait_rec1"):
        await_halo(6, (2, 3, 3))
        await_halo(1, (2, 3, 3), sems=send_sem)

    def add_samples(x, carry):
        ext = pl.ds(BASE, wide)
        waves[1][1][0, x, ext] = waves[1][1][0, x, ext] + samples_at(STEPS - 1, x, 0, wide)
        return carry

    with scope("add_samples"):
        lax.fori_loop(0, nx + 2 * DEEP, add_samples, 0, unroll=nx + 2 * DEEP)
    for level in range(1, STEPS):
        with scope("rec_step%d" % level):
            step(1, level)

    def finish(beside_x, beside_y):
        total = packed * (n - 1)
        for group in ((4, 1, 2), (5, 2, 2), (4, 1, 0), (2, 3, 3)):
            total += halo_rows(*group, beside_x, beside_y)
        if total:
            await_rows(send_sem.at[0], total)

    with scope("finish"):
        by_place(finish)


def write_out(*refs):
    values, results, done = refs[:3], refs[3:6], refs[6]
    copies = [pltpu.make_async_copy(values[i], results[i], done.at[i]) for i in range(3)]
    for copy in copies:
        copy.start()
    for copy in copies:
        copy.wait()


def per_device(*args):
    nx, ny, nz = args[0].shape
    n_gx, n_gy = lax.axis_size("gx"), lax.axis_size("gy")
    traces, receiver_x, receiver_y, segment_start = args[13:]
    samples, local_rec = traces.shape
    n_rec = receiver_x.shape[0]
    n = n_gx * n_gy
    sizes = (n_gx, n_gy, nx, ny, nz, local_rec, n_rec)
    positions = [r.reshape(n_rec // LANES, LANES) for r in (receiver_x, receiver_y)]
    anywhere = pl.BlockSpec(memory_space=pltpu.HBM)
    block = jax.ShapeDtypeStruct((nx, ny, nz), jnp.float32)
    held = pltpu.VMEM((nx, ny, nz), jnp.float32)
    ends = pl.pallas_call(
        functools.partial(kernel, sizes),
        out_shape=(held,) * 3,
        in_specs=[anywhere] * 16 + [pl.BlockSpec(memory_space=pltpu.SMEM)],
        out_specs=(pl.BlockSpec(memory_space=pltpu.VMEM),) * 3,
        scratch_shapes=[
            *[pltpu.VMEM((2, nx + 2 * DEEP, ny + 2 * TOP, nz), jnp.float32)] * (2 * STEPS + 2),
            *[pltpu.VMEM((2, nx, ny + 8, nz), jnp.float32)] * 2,
            pltpu.VMEM((13, nx + 2 * DEEP, ny + 8, nz), jnp.float32),
            pltpu.VMEM((5, nx, ny, nz), jnp.float32),
            pltpu.VMEM((5, nx + 2 * DEEP, ny + 2 * TOP, nz), jnp.float32),
            pltpu.VMEM((STEPS, ny + 8, LANES), jnp.float32),
            pltpu.VMEM((samples, local_rec), jnp.float32),
            pltpu.VMEM((8, LANES), jnp.float32),
            pltpu.VMEM((n * 8, LANES), jnp.float32),
            pltpu.VMEM((2, n_rec // LANES, LANES), jnp.int32),
            pltpu.VMEM((LANES, n_rec), jnp.float32),
            pltpu.VMEM((ny + 8, n_rec), jnp.float32),
            pltpu.VMEM((16 * n + 48 * (nx + 4) * (ny + 4), LANES), jnp.float32),
            pltpu.SemaphoreType.DMA((6,)),
            pltpu.SemaphoreType.DMA((2,)),
            pltpu.SemaphoreType.DMA((8,)),
            pltpu.SemaphoreType.REGULAR((max(n_gx, n_gy, 3) - 2,)),
        ],
        compiler_params=pltpu.CompilerParams(
            collective_id=0, has_side_effects=True, vmem_limit_bytes=48 * 1024 * 1024
        ),
        name="window",
    )(*[pltpu.with_memory_space_constraint(a, pltpu.HBM) for a in (*args[:13], traces, *positions)], segment_start)
    return pl.pallas_call(
        write_out,
        out_shape=(block,) * 3,
        in_specs=[pl.BlockSpec(memory_space=pltpu.VMEM)] * 3,
        out_specs=(pl.BlockSpec(memory_space=pltpu.HBM),) * 3,
        scratch_shapes=[pltpu.SemaphoreType.DMA((3,))],
        compiler_params=pltpu.CompilerParams(vmem_limit_bytes=1024 * 1024),
        name="write_out",
    )(*[pltpu.with_memory_space_constraint(end, pltpu.VMEM) for end in ends])


def solution(mesh):
    block, cell = P(("shot", "gx"), "gy", None), P("gx", "gy", None)
    return jax.shard_map(
        per_device,
        mesh=mesh,
        in_specs=(block,) * 8 + (cell,) * 5 + (P("shot", ("gx", "gy")), P(), P(), P()),
        out_specs=(block,) * 3,
        check_vma=False,
    )
```

```python
import functools

import jax
import jax.numpy as jnp
from jax import lax
from jax.experimental import pallas as pl
from jax.experimental.pallas import tpu as pltpu
from jax.sharding import PartitionSpec as P

STEPS = 4
REC_DEPTH = 4
DEEP = 3
RINGS = (0, 2, 1, 0)
BASE = 8
TOP = 12
LANES = 128
TILE = 8
SIDES = ((0, -1), (0, 1), (-1, 0), (1, 0), (-1, -1), (-1, 1), (1, -1), (1, 1))
MESH = pl.DeviceIdType.MESH
scope = jax.named_scope


def sine(x):
    s = x * x
    c = 1.6059044e-10
    for k in (-2.5052108e-8, 2.7557319e-6, -1.98412698e-4, 8.3333333e-3, -1.66666667e-1):
        c = c * s + k
    return x + x * (s * c)


def cosine(x):
    s = x * x
    c = -1.1470746e-11
    for k in (2.0876757e-9, -2.7557319e-7, 2.4801587e-5, -1.38888889e-3, 4.16666667e-2, -0.5):
        c = c * s + k
    return 1.0 + s * c


def kernel(sizes, *refs):
    n_gx, n_gy, nx, ny, nz, local_rec, n_rec = sizes
    fields, model = refs[:8], refs[8:13]
    traces, rec_x, rec_y, start = refs[13:17]
    image, p_last, q_last = refs[17:20]
    (*held, old_0, old_1, coef, earth, unit, inject, rows, window, gathered, rec_pos, hot_x, hot_y, pool,
     load_sem, send_sem, recv_sem, ready) = refs[20:]
    waves = (held[:STEPS + 1], held[STEPS + 1:])
    olds = (old_0, old_1)
    wide = ny + 8
    n = n_gx * n_gy
    gx, gy = lax.axis_index("gx"), lax.axis_index("gy")
    me = gx * n_gy + gy

    barrier = pltpu.get_barrier_semaphore()

    def peer_id(i):
        peer = lax.rem(me + n - i, n)
        return {"gx": peer // n_gy, "gy": lax.rem(peer, n_gy)}

    def await_rows(sem, count):
        part = pool.at[pl.ds(0, count)]
        pltpu.make_async_copy(part, part, sem).wait()

    inner_x, inner_y = pl.ds(DEEP, nx), pl.ds(TOP, ny)

    with scope("loads"):
        for g in range(2):
            for f in range(2):
                pltpu.make_async_copy(
                    fields[4 * g + 2 * f + 1], waves[g][0].at[f, inner_x, inner_y], load_sem.at[0]
                ).start()
        for i in range(5):
            pltpu.make_async_copy(model[i], earth.at[i], load_sem.at[1]).start()
        load_traces = pltpu.make_async_copy(traces, rows, load_sem.at[2])
        load_traces.start()

    def there(dx, dy):
        ok = None
        for d, pos, count in ((dx, gx, n_gx), (dy, gy, n_gy)):
            if d:
                test = pos + d < count if d > 0 else pos + d >= 0
                ok = test if ok is None else ok & test
        return ok

    def tell_neighbours(sem):
        for dx, dy in SIDES:
            @pl.when(there(dx, dy))
            def _():
                pl.semaphore_signal(
                    sem, inc=1, device_id={"gx": gx + dx, "gy": gy + dy}, device_id_type=MESH
                )

    def count_beside(pos, count):
        return jnp.where(pos > 0, 1, 0) + jnp.where(pos < count - 1, 1, 0)

    neighbours = (1 + count_beside(gx, n_gx)) * (1 + count_beside(gy, n_gy)) - 1
    rounds = max(n_gx, n_gy) - 2

    def hear_neighbours(sem):
        pl.semaphore_wait(sem, neighbours)

    def tell_above(i, carry):
        ahead, peer_x = 1 + i // n_gx, lax.rem(i, n_gx)
        apart = jnp.where(peer_x > gx, peer_x - gx, gx - peer_x)

        @pl.when((gy + ahead < n_gy) & ((ahead > 1) | (apart > 1)))
        def _():
            pl.semaphore_signal(
                barrier, inc=1, device_id={"gx": peer_x, "gy": gy + ahead}, device_id_type=MESH
            )

        return carry

    with scope("greet"):
        tell_neighbours(barrier)
        above = n_gx * (n_gy - 1)
        if above:
            lax.fori_loop(0, above, tell_above, 0, unroll=min(12, above))

    def span(d, start, size, first, last):
        if d == 0:
            return pl.ds(start, size), pl.ds(start, size)
        if d > 0:
            return pl.ds(start + size - last, last - first), pl.ds(start - last, last - first)
        return pl.ds(start + first, last - first), pl.ds(start + size + first, last - first)

    def send(ref, slot, near, far, corner, out=0):
        for dx, dy in SIDES:
            first, last = (0, corner) if dx and dy else (near, far)
            if last == first:
                continue

            @pl.when(there(dx, dy))
            def _():
                src_x, dst_x = span(dx, DEEP, nx, first, last)
                src_y, dst_y = span(dy, TOP, ny, first, last)
                pltpu.make_async_remote_copy(
                    src_ref=ref.at[:, src_x, src_y],
                    dst_ref=ref.at[:, dst_x, dst_y],
                    send_sem=send_sem.at[out],
                    recv_sem=recv_sem.at[slot],
                    device_id={"gx": gx + dx, "gy": gy + dy},
                    device_id_type=MESH,
                ).start()

    def halo_rows(count, layers, corner, beside_x, beside_y):
        faces = beside_x * ny + beside_y * nx
        return count * (layers * faces + beside_x * beside_y * corner * corner)

    def by_place(act):
        for beside_x in range(min(n_gx, 3)):
            for beside_y in range(min(n_gy, 3)):
                here_x = jnp.where(gx > 0, 1, 0) + jnp.where(gx < n_gx - 1, 1, 0) == beside_x
                here_y = jnp.where(gy > 0, 1, 0) + jnp.where(gy < n_gy - 1, 1, 0) == beside_y

                @pl.when(here_x & here_y)
                def _():
                    act(beside_x, beside_y)

    def await_halo(slot, *groups, sems=recv_sem):
        def act(beside_x, beside_y):
            total = sum(halo_rows(*group, beside_x, beside_y) for group in groups)
            if total:
                await_rows(sems.at[slot], total)

        by_place(act)

    with scope("wait_now"):
        await_rows(load_sem.at[0], 4 * nx * ny)
    with scope("barrier"):
        beside = count_beside(gx, n_gx)
        pl.semaphore_wait(barrier, n_gx * gy + beside + jnp.where(gy < n_gy - 1, 1 + beside, 0))
    with scope("send_src0"):
        if rounds > 0:
            tell_neighbours(ready.at[0])
        send(waves[0][0], 0, 0, 1, 2)
        send(waves[1][0], 1, 0, 1, 2)

    per_row = LANES // local_rec
    packed = STEPS // per_row
    with scope("window"):
        load_traces.wait()
        window[...] = jnp.zeros_like(window)
        window[0:STEPS, 0:local_rec] = rows[pl.ds(start[0], STEPS), :]
        sample = window[...]
        for r in range(packed):
            row = sample[r * per_row:r * per_row + 1]
            for j in range(1, per_row):
                row = row + pltpu.roll(sample[r * per_row + j:r * per_row + j + 1], j * local_rec, 1)
            window[r:r + 1] = row
        mine = pl.ds(pl.multiple_of(me * 8, 8), packed)
        gathered[mine] = window[0:packed]

    def far_start(lower, i, carry):
        peer_x, peer_y = i // n_gy, lax.rem(i, n_gy)
        chosen = peer_y < gy if lower else (peer_y >= gy) & (i != me)

        @pl.when(chosen)
        def _():
            pltpu.make_async_remote_copy(
                src_ref=window.at[0:packed],
                dst_ref=gathered.at[mine],
                send_sem=send_sem.at[0],
                recv_sem=recv_sem.at[7],
                device_id={"gx": peer_x, "gy": peer_y},
                device_id_type=MESH,
            ).start()

        return carry

    with scope("far_below"):
        lax.fori_loop(0, n, functools.partial(far_start, True), 0, unroll=min(16, n))

    with scope("wait_model"):
        await_rows(load_sem.at[1], 5 * nx * ny)

    def units(x, carry):
        v = earth[0, x]
        f_e = 1.0 + 2.0 * earth[1, x]
        f_d = jnp.sqrt(1.0 + 2.0 * earth[2, x])
        tilt = earth[3, x]
        half = 0.5 * earth[4, x]
        sin_t = sine(tilt)
        sin_h, cos_h = sine(half), cosine(half)
        sin_a = 2.0 * sin_h * cos_h
        cos_a = 1.0 - 2.0 * sin_h * sin_h
        to = (x + DEEP, inner_y)
        unit[(0, *to)] = v
        unit[(1, *to)] = v * f_e
        unit[(2, *to)] = v * f_d
        unit[(3, *to)] = sin_t * cos_a
        unit[(4, *to)] = sin_t * sin_a
        return carry

    with scope("units"):
        lax.fori_loop(0, nx, units, 0, unroll=nx)

    with scope("send_model"):
        send(unit, 2, 0, 2, 2)
    with scope("send_layer"):
        send(waves[0][0], 3, 1, 2, 0)
        send(waves[1][0], 4, 1, 2, 0)
    for g in range(2):
        for f in range(2):
            pltpu.make_async_copy(
                fields[4 * g + 2 * f], olds[g].at[f, :, pl.ds(TOP - BASE, ny)], load_sem.at[3]
            ).start()
    load_x = pltpu.make_async_copy(rec_x, rec_pos.at[0], load_sem.at[4])
    load_y = pltpu.make_async_copy(rec_y, rec_pos.at[1], load_sem.at[5])
    load_x.start()
    load_y.start()

    with scope("round"):
        if rounds > 0:
            hear_neighbours(ready.at[0])
        if rounds > 1:
            tell_neighbours(ready.at[1])

    def clear(ref, count, depth):
        zeros = jnp.zeros((wide, nz), jnp.float32)
        for edge, first in ((gx == 0, DEEP - depth), (gx == n_gx - 1, DEEP + nx)):
            @pl.when(edge)
            def _():
                for f in range(count):
                    for x in range(first, first + depth):
                        ref[f, x, BASE:BASE + wide] = zeros
        for edge, first in ((gy == 0, TOP - depth), (gy == n_gy - 1, TOP + ny)):
            @pl.when(edge)
            def _():
                for f in range(count):
                    ref[f, :, first:first + depth] = jnp.zeros((nx + 2 * DEEP, depth, nz), jnp.float32)

    with scope("clear"):
        for g in range(2):
            clear(waves[g][0], 2, 2)
            clear(waves[g][1], 2, 3)
        clear(unit, 5, 2)

    def after(value):
        return pltpu.roll(value, nz - 1, 1)

    def before(value):
        return pltpu.roll(value, 1, 1)

    def factors(x, first, count):
        lane = lax.broadcasted_iota(jnp.int32, (count, nz), 1)
        at = pl.ds(first, count)
        to = pl.ds(first - BASE, count)
        n_x, n_y = unit[3, x, at], unit[4, x, at]
        a_xx, a_yy = n_x * n_x, n_y * n_y
        a_zz = 1.0 - (a_xx + a_yy)
        half_z = 0.5 * jnp.sqrt(a_zz)
        a_xz, a_yz = half_z * n_x, half_z * n_y
        coef[0, x, to] = a_xx
        coef[1, x, to] = a_yy
        coef[4, x, to] = 1.0 - a_xx
        coef[5, x, to] = 1.0 - a_yy
        coef[8, x, to] = (0.5 * n_x) * n_y
        for shift, edge, i in ((before, lane == 0, 0), (after, lane == nz - 1, 1)):
            moved = shift(a_zz)
            coef[2 + i, x, to] = jnp.where(edge, 0.0, moved)
            coef[6 + i, x, to] = jnp.where(edge, 0.0, 1.0 - moved)
            coef[9 + 2 * i, x, to] = jnp.where(edge, 0.0, shift(a_xz))
            coef[10 + 2 * i, x, to] = jnp.where(edge, 0.0, shift(a_yz))

    def inner_factors(x, carry):
        factors(x, TOP, ny)
        return carry

    def outer_factors(x, carry):
        factors(x, BASE, 8)
        factors(x, BASE + wide - 8, 8)
        return carry

    with scope("inner_factors"):
        lax.fori_loop(DEEP, DEEP + nx, inner_factors, 0, unroll=nx)

    def around(now, f, x, lo, count):
        center = now[f, x, pl.ds(lo, count)]
        y_up, y_down = now[f, x, pl.ds(lo + 1, count)], now[f, x, pl.ds(lo - 1, count)]
        return center, y_up - y_down, y_up + y_down

    def rotated(planes, x, at, weights):
        sign, w_x, w_y, w_up, w_down = weights
        (x_down, dy_down, _), (center, d_y, s_y), (x_up, dy_up, _) = planes
        d_x, d_xy = x_up - x_down, dy_up - dy_down
        flat = coef[w_x, x, at] * (x_up + x_down) + coef[w_y, x, at] * s_y
        mixed = coef[8, x, at] * d_xy
        above, below = coef[w_up, x, at] * center, coef[w_down, x, at] * center
        mixed_above = coef[9, x, at] * d_x + coef[10, x, at] * d_y
        mixed_below = coef[11, x, at] * d_x + coef[12, x, at] * d_y
        if sign > 0:
            return (flat + mixed) + (after(above + mixed_above) + before(below - mixed_below))
        return (flat - mixed) + (after(above - mixed_above) + before(below + mixed_below))

    def step(g, level, part=None):
        ring = RINGS[level]
        first, last = DEEP - ring, DEEP + nx + ring
        if part is None:
            plane_range(g, level, first, last, BASE if ring else TOP, wide if ring else ny)
            return
        lo, count, margin = (TOP + 1, ny - 2, 1) if level == 1 else (TOP + 4, ny - 8, 2)
        if part == "inner":
            plane_range(g, level, DEEP + margin, DEEP + nx - margin, lo, count)
        else:
            for edge in ((first, DEEP + margin), (DEEP + nx - margin, last)):
                plane_range(g, level, *edge, BASE, wide)
            for start in (BASE, BASE + wide - 8):
                plane_range(g, level, DEEP + margin, DEEP + nx - margin, start, 8)

    def plane_range(g, level, first, last, lo, count):
        for start in range(lo, lo + count, TILE):
            tile_range(g, level, first, last, start, min(TILE, lo + count - start))

    def tile_range(g, level, first, last, lo, count):
        now, later = waves[g][level], waves[g][level + 1] if g == 0 or level < STEPS - 1 else None
        mid, at = pl.ds(lo, count), pl.ds(lo - BASE, count)

        def plane(x, carry):
            p_planes, q_planes = [[*carry[f], around(now, f, x + 1, lo, count)] for f in range(2)]
            p_now, q_now = p_planes[1][0], q_planes[1][0]
            p_two, q_two = p_now + p_now, q_now + q_now
            across = rotated(p_planes, x, at, (-1, 4, 5, 6, 7)) - (p_two + p_two)
            q_axis = rotated(q_planes, x, at, (1, 0, 1, 2, 3)) - q_two
            v_d = unit[2, x, mid]
            if level:
                p_prev, q_prev = waves[g][level - 1][0, x, mid], waves[g][level - 1][1, x, mid]
            else:
                p_prev, q_prev = olds[g][0, x - DEEP, at], olds[g][1, x - DEEP, at]
            p_next = (p_two - p_prev) + (unit[1, x, mid] * across + v_d * q_axis)
            if g == 1 and level:
                p_next = p_next + samples_at(STEPS - 1 - level, x, lo - BASE, count)
            carry = (tuple(p_planes[1:]), tuple(q_planes[1:]))
            if g == 0 and level == STEPS - 1:
                later[0, x, mid] = p_next
                return carry
            q_next = (q_two - q_prev) + (v_d * across + unit[0, x, mid] * q_axis)
            if g == 1 and level == STEPS - 1:
                to = pl.ds(lo - TOP, count)
                p_last[x - DEEP, to] = p_next
                q_last[x - DEEP, to] = q_next
                total = waves[0][0][0, x, mid] * p_next
                for k in range(STEPS):
                    total = total + waves[1][k][0, x, mid] * waves[0][STEPS - k][0, x, mid]
                image[x - DEEP, to] = total
            else:
                later[0, x, mid] = p_next
                later[1, x, mid] = q_next
            return carry

        begin = tuple(tuple(around(now, f, x, lo, count) for x in (first - 1, first)) for f in range(2))
        lax.fori_loop(first, last, plane, begin, unroll=last - first)

    n_rows = n_rec // LANES
    wide_x = hot_x.shape[0]

    def find(i, carry):
        to = pl.ds(pl.multiple_of(i * LANES, LANES), LANES)
        x_id = lax.broadcasted_iota(jnp.int32, (wide_x, LANES), 0) + (gx * nx - DEEP)
        y_id = lax.broadcasted_iota(jnp.int32, (wide, LANES), 0) + (gy * ny - (TOP - BASE))
        hot_x[:, to] = jnp.where(rec_pos[0, pl.ds(i, 1)] == x_id, 1.0, 0.0)
        hot_y[:, to] = jnp.where(rec_pos[1, pl.ds(i, 1)] == y_id, 1.0, 0.0)
        return carry

    with scope("find"):
        load_x.wait()
        load_y.wait()
        lax.fori_loop(0, n_rows, find, 0, unroll=8)

    def make_planes():
        segment = lax.broadcasted_iota(jnp.int32, (n_rows, LANES), 1) // local_rec
        parts = []
        for k in range(STEPS):
            r, own = k // per_row, k % per_row
            sample = None
            for j in range(per_row):
                piece = gathered[pl.ds(j * 8 + r, n_rows, stride=per_row * 8), :]
                piece = jnp.where(segment == own, piece, 0.0)
                if j != own:
                    piece = pltpu.roll(piece, (j - own) * local_rec % LANES, 1)
                sample = piece if sample is None else sample + piece
            for _ in range(3):
                part = sample.astype(jnp.bfloat16).astype(jnp.float32)
                parts.append(part)
                sample = sample - part
        chunk = min(8, n_rows)
        total = jnp.zeros((3 * STEPS * wide, wide_x), jnp.float32)
        for base in range(0, n_rows, chunk):
            columns = slice(base * LANES, (base + chunk) * LANES)
            left = jnp.concatenate(
                [
                    jnp.concatenate(
                        [hot_y[:, i * LANES:(i + 1) * LANES] * part[i:i + 1] for part in parts], axis=0
                    )
                    for i in range(base, base + chunk)
                ],
                axis=1,
            )
            total = total + lax.dot_general(
                left, hot_x[:, columns], (((1,), (1,)), ((), ())), preferred_element_type=jnp.float32
            )
        for k in range(STEPS):
            three = [total[(3 * k + i) * wide:(3 * k + i + 1) * wide] for i in range(3)]
            inject[k] = (three[0] + three[1]) + three[2]

    def samples_at(k, x, first, count):
        lane = lax.broadcasted_iota(jnp.int32, (count, LANES), 1)
        column = pltpu.roll(inject[k, pl.ds(first, count)], lax.rem(LANES + REC_DEPTH - x, LANES), 1)
        return jnp.where(lane == REC_DEPTH, column, 0.0)

    with scope("rounds"):
        for i in range(1, rounds):
            hear_neighbours(ready.at[i])
            if i + 1 < rounds:
                tell_neighbours(ready.at[i + 1])
    with scope("far_rest"):
        lax.fori_loop(0, n, functools.partial(far_start, False), 0, unroll=min(16, n))
    with scope("wait_prev"):
        await_rows(load_sem.at[3], 4 * nx * ny)
    with scope("wait_src0"):
        await_halo(0, (2, 1, 2))
    with scope("src_step0"):
        step(0, 0)
    with scope("send_src1"):
        send(waves[0][1], 5, 0, 3, 3)
    with scope("wait_rec0"):
        await_halo(1, (2, 1, 2))
    with scope("rec_step0"):
        step(1, 0)
    with scope("send_rec1"):
        send(waves[1][1], 6, 0, 3, 3, out=1)
    with scope("wait_model_halo"):
        await_halo(2, (5, 2, 2))
    with scope("outer_factors"):
        lax.fori_loop(DEEP, DEEP + nx, outer_factors, 0, unroll=nx)
        for x in (DEEP - 2, DEEP - 1, DEEP + nx, DEEP + nx + 1):
            factors(x, BASE, wide)
    with scope("src_inner"):
        for level in (1, 2):
            step(0, level, "inner")
    with scope("wait_far"):
        if n > 1:
            await_rows(recv_sem.at[7], packed * (n - 1))
    with scope("planes"):
        make_planes()
    with scope("wait_src1"):
        await_halo(3, (2, 1, 0))
        await_halo(5, (2, 3, 3))
    for level in range(1, STEPS):
        with scope("src_step%d" % level):
            step(0, level, "outer" if level < STEPS - 1 else None)
    with scope("wait_rec1"):
        await_halo(4, (2, 1, 0))
        await_halo(6, (2, 3, 3))
        await_halo(1, (2, 3, 3), sems=send_sem)

    def add_samples(x, carry):
        ext = pl.ds(BASE, wide)
        waves[1][1][0, x, ext] = waves[1][1][0, x, ext] + samples_at(STEPS - 1, x, 0, wide)
        return carry

    with scope("add_samples"):
        lax.fori_loop(0, nx + 2 * DEEP, add_samples, 0, unroll=nx + 2 * DEEP)
    for level in range(1, STEPS):
        with scope("rec_step%d" % level):
            step(1, level)

    def finish(beside_x, beside_y):
        total = packed * (n - 1)
        for group in ((4, 1, 2), (5, 2, 2), (4, 1, 0), (2, 3, 3)):
            total += halo_rows(*group, beside_x, beside_y)
        if total:
            await_rows(send_sem.at[0], total)

    with scope("finish"):
        by_place(finish)


def write_out(*refs):
    values, results, done = refs[:3], refs[3:6], refs[6]
    copies = [pltpu.make_async_copy(values[i], results[i], done.at[i]) for i in range(3)]
    for copy in copies:
        copy.start()
    for copy in copies:
        copy.wait()


def per_device(*args):
    nx, ny, nz = args[0].shape
    n_gx, n_gy = lax.axis_size("gx"), lax.axis_size("gy")
    traces, receiver_x, receiver_y, segment_start = args[13:]
    samples, local_rec = traces.shape
    n_rec = receiver_x.shape[0]
    n = n_gx * n_gy
    sizes = (n_gx, n_gy, nx, ny, nz, local_rec, n_rec)
    positions = [r.reshape(n_rec // LANES, LANES) for r in (receiver_x, receiver_y)]
    anywhere = pl.BlockSpec(memory_space=pltpu.HBM)
    block = jax.ShapeDtypeStruct((nx, ny, nz), jnp.float32)
    held = pltpu.VMEM((nx, ny, nz), jnp.float32)
    ends = pl.pallas_call(
        functools.partial(kernel, sizes),
        out_shape=(held,) * 3,
        in_specs=[anywhere] * 16 + [pl.BlockSpec(memory_space=pltpu.SMEM)],
        out_specs=(pl.BlockSpec(memory_space=pltpu.VMEM),) * 3,
        scratch_shapes=[
            *[pltpu.VMEM((2, nx + 2 * DEEP, ny + 2 * TOP, nz), jnp.float32)] * (2 * STEPS + 2),
            *[pltpu.VMEM((2, nx, ny + 8, nz), jnp.float32)] * 2,
            pltpu.VMEM((13, nx + 2 * DEEP, ny + 8, nz), jnp.float32),
            pltpu.VMEM((5, nx, ny, nz), jnp.float32),
            pltpu.VMEM((5, nx + 2 * DEEP, ny + 2 * TOP, nz), jnp.float32),
            pltpu.VMEM((STEPS, ny + 8, LANES), jnp.float32),
            pltpu.VMEM((samples, local_rec), jnp.float32),
            pltpu.VMEM((8, LANES), jnp.float32),
            pltpu.VMEM((n * 8, LANES), jnp.float32),
            pltpu.VMEM((2, n_rec // LANES, LANES), jnp.int32),
            pltpu.VMEM((LANES, n_rec), jnp.float32),
            pltpu.VMEM((ny + 8, n_rec), jnp.float32),
            pltpu.VMEM((16 * n + 48 * (nx + 4) * (ny + 4), LANES), jnp.float32),
            pltpu.SemaphoreType.DMA((6,)),
            pltpu.SemaphoreType.DMA((2,)),
            pltpu.SemaphoreType.DMA((8,)),
            pltpu.SemaphoreType.REGULAR((max(n_gx, n_gy, 3) - 2,)),
        ],
        compiler_params=pltpu.CompilerParams(
            collective_id=0, has_side_effects=True, vmem_limit_bytes=48 * 1024 * 1024
        ),
        name="window",
    )(*[pltpu.with_memory_space_constraint(a, pltpu.HBM) for a in (*args[:13], traces, *positions)], segment_start)
    return pl.pallas_call(
        write_out,
        out_shape=(block,) * 3,
        in_specs=[pl.BlockSpec(memory_space=pltpu.VMEM)] * 3,
        out_specs=(pl.BlockSpec(memory_space=pltpu.HBM),) * 3,
        scratch_shapes=[pltpu.SemaphoreType.DMA((3,))],
        compiler_params=pltpu.CompilerParams(vmem_limit_bytes=1024 * 1024),
        name="write_out",
    )(*[pltpu.with_memory_space_constraint(end, pltpu.VMEM) for end in ends])


def solution(mesh):
    block, cell = P(("shot", "gx"), "gy", None), P("gx", "gy", None)
    return jax.shard_map(
        per_device,
        mesh=mesh,
        in_specs=(block,) * 8 + (cell,) * 5 + (P("shot", ("gx", "gy")), P(), P(), P()),
        out_specs=(block,) * 3,
        check_vma=False,
    )
```

```python
import functools

import jax
import jax.numpy as jnp
from jax import lax
from jax.experimental import pallas as pl
from jax.experimental.pallas import tpu as pltpu
from jax.sharding import PartitionSpec as P

STEPS = 4
REC_DEPTH = 4
DEEP = 3
RINGS = (0, 2, 1, 0)
BASE = 8
TOP = 12
LANES = 128
TILE = 8
SIDES = ((0, -1), (0, 1), (-1, 0), (1, 0), (-1, -1), (-1, 1), (1, -1), (1, 1))
MESH = pl.DeviceIdType.MESH
scope = jax.named_scope


def sine(x):
    s = x * x
    c = 1.6059044e-10
    for k in (-2.5052108e-8, 2.7557319e-6, -1.98412698e-4, 8.3333333e-3, -1.66666667e-1):
        c = c * s + k
    return x + x * (s * c)


def cosine(x):
    s = x * x
    c = -1.1470746e-11
    for k in (2.0876757e-9, -2.7557319e-7, 2.4801587e-5, -1.38888889e-3, 4.16666667e-2, -0.5):
        c = c * s + k
    return 1.0 + s * c


def kernel(sizes, *refs):
    n_gx, n_gy, nx, ny, nz, local_rec, n_rec = sizes
    fields, model = refs[:8], refs[8:13]
    traces, rec_x, rec_y, start = refs[13:17]
    image, p_last, q_last = refs[17:20]
    (*held, old_0, old_1, coef, earth, unit, inject, rows, window, gathered, rec_pos, hot_x, hot_y, pool,
     load_sem, send_sem, recv_sem, ready) = refs[20:]
    waves = (held[:STEPS + 1], held[STEPS + 1:])
    olds = (old_0, old_1)
    wide = ny + 8
    n = n_gx * n_gy
    gx, gy = lax.axis_index("gx"), lax.axis_index("gy")
    me = gx * n_gy + gy

    barrier = pltpu.get_barrier_semaphore()

    def peer_id(i):
        peer = lax.rem(me + n - i, n)
        return {"gx": peer // n_gy, "gy": lax.rem(peer, n_gy)}

    def await_rows(sem, count):
        part = pool.at[pl.ds(0, count)]
        pltpu.make_async_copy(part, part, sem).wait()

    inner_x, inner_y = pl.ds(DEEP, nx), pl.ds(TOP, ny)

    with scope("loads"):
        for g in range(2):
            for f in range(2):
                pltpu.make_async_copy(
                    fields[4 * g + 2 * f + 1], waves[g][0].at[f, inner_x, inner_y], load_sem.at[0]
                ).start()
        for i in range(5):
            pltpu.make_async_copy(model[i], earth.at[i], load_sem.at[1]).start()
        load_traces = pltpu.make_async_copy(traces, rows, load_sem.at[2])
        load_traces.start()

    def there(dx, dy):
        ok = None
        for d, pos, count in ((dx, gx, n_gx), (dy, gy, n_gy)):
            if d:
                test = pos + d < count if d > 0 else pos + d >= 0
                ok = test if ok is None else ok & test
        return ok

    def tell_neighbours(sem):
        for dx, dy in SIDES:
            @pl.when(there(dx, dy))
            def _():
                pl.semaphore_signal(
                    sem, inc=1, device_id={"gx": gx + dx, "gy": gy + dy}, device_id_type=MESH
                )

    def count_beside(pos, count):
        return jnp.where(pos > 0, 1, 0) + jnp.where(pos < count - 1, 1, 0)

    neighbours = (1 + count_beside(gx, n_gx)) * (1 + count_beside(gy, n_gy)) - 1
    rounds = max(n_gx, n_gy) - 2

    def hear_neighbours(sem):
        pl.semaphore_wait(sem, neighbours)

    def tell_above(i, carry):
        ahead, peer_x = 1 + i // n_gx, lax.rem(i, n_gx)
        apart = jnp.where(peer_x > gx, peer_x - gx, gx - peer_x)

        @pl.when((gy + ahead < n_gy) & ((ahead > 1) | (apart > 1)))
        def _():
            pl.semaphore_signal(
                barrier, inc=1, device_id={"gx": peer_x, "gy": gy + ahead}, device_id_type=MESH
            )

        return carry

    with scope("greet"):
        tell_neighbours(barrier)
        above = n_gx * (n_gy - 1)
        if above:
            lax.fori_loop(0, above, tell_above, 0, unroll=min(12, above))

    def span(d, start, size, first, last):
        if d == 0:
            return pl.ds(start, size), pl.ds(start, size)
        if d > 0:
            return pl.ds(start + size - last, last - first), pl.ds(start - last, last - first)
        return pl.ds(start + first, last - first), pl.ds(start + size + first, last - first)

    def send(ref, slot, near, far, corner, out=0):
        for dx, dy in SIDES:
            first, last = (0, corner) if dx and dy else (near, far)
            if last == first:
                continue

            @pl.when(there(dx, dy))
            def _():
                src_x, dst_x = span(dx, DEEP, nx, first, last)
                src_y, dst_y = span(dy, TOP, ny, first, last)
                pltpu.make_async_remote_copy(
                    src_ref=ref.at[:, src_x, src_y],
                    dst_ref=ref.at[:, dst_x, dst_y],
                    send_sem=send_sem.at[out],
                    recv_sem=recv_sem.at[slot],
                    device_id={"gx": gx + dx, "gy": gy + dy},
                    device_id_type=MESH,
                ).start()

    def halo_rows(count, layers, corner, beside_x, beside_y):
        faces = beside_x * ny + beside_y * nx
        return count * (layers * faces + beside_x * beside_y * corner * corner)

    def by_place(act):
        for beside_x in range(min(n_gx, 3)):
            for beside_y in range(min(n_gy, 3)):
                here_x = jnp.where(gx > 0, 1, 0) + jnp.where(gx < n_gx - 1, 1, 0) == beside_x
                here_y = jnp.where(gy > 0, 1, 0) + jnp.where(gy < n_gy - 1, 1, 0) == beside_y

                @pl.when(here_x & here_y)
                def _():
                    act(beside_x, beside_y)

    def await_halo(slot, *groups, sems=recv_sem):
        def act(beside_x, beside_y):
            total = sum(halo_rows(*group, beside_x, beside_y) for group in groups)
            if total:
                await_rows(sems.at[slot], total)

        by_place(act)

    with scope("wait_now"):
        await_rows(load_sem.at[0], 4 * nx * ny)
    with scope("barrier"):
        beside = count_beside(gx, n_gx)
        pl.semaphore_wait(barrier, n_gx * gy + beside + jnp.where(gy < n_gy - 1, 1 + beside, 0))
    with scope("send_src0"):
        if rounds > 0:
            tell_neighbours(ready.at[0])
        send(waves[0][0], 0, 0, 1, 2)
        send(waves[1][0], 1, 0, 1, 2)

    per_row = LANES // local_rec
    packed = STEPS // per_row
    with scope("window"):
        load_traces.wait()
        window[...] = jnp.zeros_like(window)
        window[0:STEPS, 0:local_rec] = rows[pl.ds(start[0], STEPS), :]
        sample = window[...]
        for r in range(packed):
            row = sample[r * per_row:r * per_row + 1]
            for j in range(1, per_row):
                row = row + pltpu.roll(sample[r * per_row + j:r * per_row + j + 1], j * local_rec, 1)
            window[r:r + 1] = row
        mine = pl.ds(pl.multiple_of(me * 8, 8), packed)
        gathered[mine] = window[0:packed]

    def far_start(lower, i, carry):
        peer_x, peer_y = i // n_gy, lax.rem(i, n_gy)
        chosen = peer_y < gy if lower else (peer_y >= gy) & (i != me)

        @pl.when(chosen)
        def _():
            pltpu.make_async_remote_copy(
                src_ref=window.at[0:packed],
                dst_ref=gathered.at[mine],
                send_sem=send_sem.at[0],
                recv_sem=recv_sem.at[7],
                device_id={"gx": peer_x, "gy": peer_y},
                device_id_type=MESH,
            ).start()

        return carry

    with scope("far_below"):
        lax.fori_loop(0, n, functools.partial(far_start, True), 0, unroll=min(16, n))

    with scope("wait_model"):
        await_rows(load_sem.at[1], 5 * nx * ny)

    def units(x, carry):
        v = earth[0, x]
        f_e = 1.0 + 2.0 * earth[1, x]
        f_d = jnp.sqrt(1.0 + 2.0 * earth[2, x])
        tilt = earth[3, x]
        half = 0.5 * earth[4, x]
        sin_t = sine(tilt)
        sin_h, cos_h = sine(half), cosine(half)
        sin_a = 2.0 * sin_h * cos_h
        cos_a = 1.0 - 2.0 * sin_h * sin_h
        to = (x + DEEP, inner_y)
        unit[(0, *to)] = v
        unit[(1, *to)] = v * f_e
        unit[(2, *to)] = v * f_d
        unit[(3, *to)] = sin_t * cos_a
        unit[(4, *to)] = sin_t * sin_a
        return carry

    with scope("units"):
        lax.fori_loop(0, nx, units, 0, unroll=nx)

    with scope("send_model"):
        send(unit, 2, 0, 2, 2)
    with scope("send_layer"):
        send(waves[0][0], 3, 1, 2, 0)
        send(waves[1][0], 4, 1, 2, 0)
    for g in range(2):
        for f in range(2):
            pltpu.make_async_copy(
                fields[4 * g + 2 * f], olds[g].at[f, :, pl.ds(TOP - BASE, ny)], load_sem.at[3]
            ).start()
    load_x = pltpu.make_async_copy(rec_x, rec_pos.at[0], load_sem.at[4])
    load_y = pltpu.make_async_copy(rec_y, rec_pos.at[1], load_sem.at[5])
    load_x.start()
    load_y.start()

    with scope("round"):
        if rounds > 0:
            hear_neighbours(ready.at[0])
        if rounds > 1:
            tell_neighbours(ready.at[1])

    def clear(ref, count, depth):
        zeros = jnp.zeros((wide, nz), jnp.float32)
        for edge, first in ((gx == 0, DEEP - depth), (gx == n_gx - 1, DEEP + nx)):
            @pl.when(edge)
            def _():
                for f in range(count):
                    for x in range(first, first + depth):
                        ref[f, x, BASE:BASE + wide] = zeros
        for edge, first in ((gy == 0, TOP - depth), (gy == n_gy - 1, TOP + ny)):
            @pl.when(edge)
            def _():
                for f in range(count):
                    ref[f, :, first:first + depth] = jnp.zeros((nx + 2 * DEEP, depth, nz), jnp.float32)

    with scope("clear"):
        for g in range(2):
            clear(waves[g][0], 2, 2)
            clear(waves[g][1], 2, 3)
        clear(unit, 5, 2)

    def after(value):
        return pltpu.roll(value, nz - 1, 1)

    def before(value):
        return pltpu.roll(value, 1, 1)

    def factors(x, first, count):
        lane = lax.broadcasted_iota(jnp.int32, (count, nz), 1)
        at = pl.ds(first, count)
        to = pl.ds(first - BASE, count)
        n_x, n_y = unit[3, x, at], unit[4, x, at]
        a_xx, a_yy = n_x * n_x, n_y * n_y
        a_zz = 1.0 - (a_xx + a_yy)
        half_z = 0.5 * jnp.sqrt(a_zz)
        a_xz, a_yz = half_z * n_x, half_z * n_y
        coef[0, x, to] = a_xx
        coef[1, x, to] = a_yy
        coef[4, x, to] = 1.0 - a_xx
        coef[5, x, to] = 1.0 - a_yy
        coef[8, x, to] = (0.5 * n_x) * n_y
        for shift, edge, i in ((before, lane == 0, 0), (after, lane == nz - 1, 1)):
            moved = shift(a_zz)
            coef[2 + i, x, to] = jnp.where(edge, 0.0, moved)
            coef[6 + i, x, to] = jnp.where(edge, 0.0, 1.0 - moved)
            coef[9 + 2 * i, x, to] = jnp.where(edge, 0.0, shift(a_xz))
            coef[10 + 2 * i, x, to] = jnp.where(edge, 0.0, shift(a_yz))

    def inner_factors(x, carry):
        factors(x, TOP, ny)
        return carry

    def outer_factors(x, carry):
        factors(x, BASE, 8)
        factors(x, BASE + wide - 8, 8)
        return carry

    with scope("inner_factors"):
        lax.fori_loop(DEEP, DEEP + nx, inner_factors, 0, unroll=nx)

    def around(now, f, x, lo, count):
        center = now[f, x, pl.ds(lo, count)]
        y_up, y_down = now[f, x, pl.ds(lo + 1, count)], now[f, x, pl.ds(lo - 1, count)]
        return center, y_up - y_down, y_up + y_down

    def rotated(planes, x, at, weights):
        sign, w_x, w_y, w_up, w_down = weights
        (x_down, dy_down, _), (center, d_y, s_y), (x_up, dy_up, _) = planes
        d_x, d_xy = x_up - x_down, dy_up - dy_down
        flat = coef[w_x, x, at] * (x_up + x_down) + coef[w_y, x, at] * s_y
        mixed = coef[8, x, at] * d_xy
        above, below = coef[w_up, x, at] * center, coef[w_down, x, at] * center
        mixed_above = coef[9, x, at] * d_x + coef[10, x, at] * d_y
        mixed_below = coef[11, x, at] * d_x + coef[12, x, at] * d_y
        if sign > 0:
            return (flat + mixed) + (after(above + mixed_above) + before(below - mixed_below))
        return (flat - mixed) + (after(above - mixed_above) + before(below + mixed_below))

    def add_range(first, last, lo, count):
        rows_here = pl.ds(lo, count)

        def add_samples(x, carry):
            new = waves[1][1][0, x, rows_here] + samples_at(STEPS - 1, x, lo - BASE, count)
            waves[1][1][0, x, rows_here] = new
            return carry

        lax.fori_loop(first, last, add_samples, 0, unroll=last - first)

    def step(g, level, part=None):
        ring = RINGS[level]
        first, last = DEEP - ring, DEEP + nx + ring
        if part is None:
            plane_range(g, level, first, last, BASE if ring else TOP, wide if ring else ny)
            return
        lo, count, margin = (TOP + 1, ny - 2, 1) if level == 1 else (TOP + 4, ny - 8, 2)
        if part == "inner":
            plane_range(g, level, DEEP + margin, DEEP + nx - margin, lo, count)
        else:
            for edge in ((first, DEEP + margin), (DEEP + nx - margin, last)):
                plane_range(g, level, *edge, BASE, wide)
            for start in (BASE, BASE + wide - 8):
                plane_range(g, level, DEEP + margin, DEEP + nx - margin, start, 8)

    def plane_range(g, level, first, last, lo, count):
        for start in range(lo, lo + count, TILE):
            tile_range(g, level, first, last, start, min(TILE, lo + count - start))

    def tile_range(g, level, first, last, lo, count):
        now, later = waves[g][level], waves[g][level + 1] if g == 0 or level < STEPS - 1 else None
        mid, at = pl.ds(lo, count), pl.ds(lo - BASE, count)

        def plane(x, carry):
            p_planes, q_planes = [[*carry[f], around(now, f, x + 1, lo, count)] for f in range(2)]
            p_now, q_now = p_planes[1][0], q_planes[1][0]
            p_two, q_two = p_now + p_now, q_now + q_now
            across = rotated(p_planes, x, at, (-1, 4, 5, 6, 7)) - (p_two + p_two)
            q_axis = rotated(q_planes, x, at, (1, 0, 1, 2, 3)) - q_two
            v_d = unit[2, x, mid]
            if level:
                p_prev, q_prev = waves[g][level - 1][0, x, mid], waves[g][level - 1][1, x, mid]
            else:
                p_prev, q_prev = olds[g][0, x - DEEP, at], olds[g][1, x - DEEP, at]
            p_next = (p_two - p_prev) + (unit[1, x, mid] * across + v_d * q_axis)
            if g == 1 and level:
                p_next = p_next + samples_at(STEPS - 1 - level, x, lo - BASE, count)
            carry = (tuple(p_planes[1:]), tuple(q_planes[1:]))
            if g == 0 and level == STEPS - 1:
                later[0, x, mid] = p_next
                return carry
            q_next = (q_two - q_prev) + (v_d * across + unit[0, x, mid] * q_axis)
            if g == 1 and level == STEPS - 1:
                to = pl.ds(lo - TOP, count)
                p_last[x - DEEP, to] = p_next
                q_last[x - DEEP, to] = q_next
                total = waves[0][0][0, x, mid] * p_next
                for k in range(STEPS):
                    total = total + waves[1][k][0, x, mid] * waves[0][STEPS - k][0, x, mid]
                image[x - DEEP, to] = total
            else:
                later[0, x, mid] = p_next
                later[1, x, mid] = q_next
            return carry

        begin = tuple(tuple(around(now, f, x, lo, count) for x in (first - 1, first)) for f in range(2))
        lax.fori_loop(first, last, plane, begin, unroll=last - first)

    n_rows = n_rec // LANES
    wide_x = hot_x.shape[0]

    def find(i, carry):
        to = pl.ds(pl.multiple_of(i * LANES, LANES), LANES)
        x_id = lax.broadcasted_iota(jnp.int32, (wide_x, LANES), 0) + (gx * nx - DEEP)
        y_id = lax.broadcasted_iota(jnp.int32, (wide, LANES), 0) + (gy * ny - (TOP - BASE))
        hot_x[:, to] = jnp.where(rec_pos[0, pl.ds(i, 1)] == x_id, 1.0, 0.0)
        hot_y[:, to] = jnp.where(rec_pos[1, pl.ds(i, 1)] == y_id, 1.0, 0.0)
        return carry

    with scope("find"):
        load_x.wait()
        load_y.wait()
        lax.fori_loop(0, n_rows, find, 0, unroll=8)

    def make_planes():
        segment = lax.broadcasted_iota(jnp.int32, (n_rows, LANES), 1) // local_rec
        parts = []
        for k in range(STEPS):
            r, own = k // per_row, k % per_row
            sample = None
            for j in range(per_row):
                piece = gathered[pl.ds(j * 8 + r, n_rows, stride=per_row * 8), :]
                piece = jnp.where(segment == own, piece, 0.0)
                if j != own:
                    piece = pltpu.roll(piece, (j - own) * local_rec % LANES, 1)
                sample = piece if sample is None else sample + piece
            for _ in range(3):
                part = sample.astype(jnp.bfloat16).astype(jnp.float32)
                parts.append(part)
                sample = sample - part
        chunk = min(8, n_rows)
        total = jnp.zeros((3 * STEPS * wide, wide_x), jnp.float32)
        for base in range(0, n_rows, chunk):
            columns = slice(base * LANES, (base + chunk) * LANES)
            left = jnp.concatenate(
                [
                    jnp.concatenate(
                        [hot_y[:, i * LANES:(i + 1) * LANES] * part[i:i + 1] for part in parts], axis=0
                    )
                    for i in range(base, base + chunk)
                ],
                axis=1,
            )
            total = total + lax.dot_general(
                left, hot_x[:, columns], (((1,), (1,)), ((), ())), preferred_element_type=jnp.float32
            )
        for k in range(STEPS):
            three = [total[(3 * k + i) * wide:(3 * k + i + 1) * wide] for i in range(3)]
            inject[k] = (three[0] + three[1]) + three[2]

    def samples_at(k, x, first, count):
        lane = lax.broadcasted_iota(jnp.int32, (count, LANES), 1)
        column = pltpu.roll(inject[k, pl.ds(first, count)], lax.rem(LANES + REC_DEPTH - x, LANES), 1)
        return jnp.where(lane == REC_DEPTH, column, 0.0)

    with scope("rounds"):
        for i in range(1, rounds):
            hear_neighbours(ready.at[i])
            if i + 1 < rounds:
                tell_neighbours(ready.at[i + 1])
    with scope("far_rest"):
        lax.fori_loop(0, n, functools.partial(far_start, False), 0, unroll=min(16, n))
    with scope("wait_prev"):
        await_rows(load_sem.at[3], 4 * nx * ny)
    with scope("wait_src0"):
        await_halo(0, (2, 1, 2))
    with scope("src_step0"):
        step(0, 0)
    with scope("send_src1"):
        send(waves[0][1], 5, 0, 3, 3)
    with scope("wait_rec0"):
        await_halo(1, (2, 1, 2))
    with scope("rec_step0"):
        step(1, 0)
    with scope("send_rec1"):
        send(waves[1][1], 6, 0, 3, 3, out=1)
    with scope("wait_model_halo"):
        await_halo(2, (5, 2, 2))
    with scope("outer_factors"):
        lax.fori_loop(DEEP, DEEP + nx, outer_factors, 0, unroll=nx)
        for x in (DEEP - 2, DEEP - 1, DEEP + nx, DEEP + nx + 1):
            factors(x, BASE, wide)
    with scope("src_inner"):
        for level in (1, 2):
            step(0, level, "inner")
    with scope("wait_far"):
        if n > 1:
            await_rows(recv_sem.at[7], packed * (n - 1))
    with scope("planes"):
        make_planes()
    with scope("rec_inner"):
        await_halo(1, (2, 3, 3), sems=send_sem)
        add_range(DEEP, DEEP + nx, TOP, ny)
        step(1, 1, "inner")
        step(1, 2, "inner")
    with scope("wait_src1"):
        await_halo(3, (2, 1, 0))
        await_halo(5, (2, 3, 3))
    for level in range(1, STEPS):
        with scope("src_step%d" % level):
            step(0, level, "outer" if level < STEPS - 1 else None)
    with scope("wait_rec1"):
        await_halo(4, (2, 1, 0))
        await_halo(6, (2, 3, 3))

    with scope("add_samples"):
        add_range(0, DEEP, BASE, wide)
        add_range(DEEP + nx, nx + 2 * DEEP, BASE, wide)
        for start in (TOP - 4, TOP + ny):
            add_range(DEEP, DEEP + nx, start, 4)

    for level in range(1, STEPS):
        with scope("rec_step%d" % level):
            step(1, level, "outer" if level < STEPS - 1 else None)

    def finish(beside_x, beside_y):
        total = packed * (n - 1)
        for group in ((4, 1, 2), (5, 2, 2), (4, 1, 0), (2, 3, 3)):
            total += halo_rows(*group, beside_x, beside_y)
        if total:
            await_rows(send_sem.at[0], total)

    with scope("finish"):
        by_place(finish)


def write_out(*refs):
    values, results, done = refs[:3], refs[3:6], refs[6]
    copies = [pltpu.make_async_copy(values[i], results[i], done.at[i]) for i in range(3)]
    for copy in copies:
        copy.start()
    for copy in copies:
        copy.wait()


def per_device(*args):
    nx, ny, nz = args[0].shape
    n_gx, n_gy = lax.axis_size("gx"), lax.axis_size("gy")
    traces, receiver_x, receiver_y, segment_start = args[13:]
    samples, local_rec = traces.shape
    n_rec = receiver_x.shape[0]
    n = n_gx * n_gy
    sizes = (n_gx, n_gy, nx, ny, nz, local_rec, n_rec)
    positions = [r.reshape(n_rec // LANES, LANES) for r in (receiver_x, receiver_y)]
    anywhere = pl.BlockSpec(memory_space=pltpu.HBM)
    block = jax.ShapeDtypeStruct((nx, ny, nz), jnp.float32)
    held = pltpu.VMEM((nx, ny, nz), jnp.float32)
    ends = pl.pallas_call(
        functools.partial(kernel, sizes),
        out_shape=(held,) * 3,
        in_specs=[anywhere] * 16 + [pl.BlockSpec(memory_space=pltpu.SMEM)],
        out_specs=(pl.BlockSpec(memory_space=pltpu.VMEM),) * 3,
        scratch_shapes=[
            *[pltpu.VMEM((2, nx + 2 * DEEP, ny + 2 * TOP, nz), jnp.float32)] * (2 * STEPS + 2),
            *[pltpu.VMEM((2, nx, ny + 8, nz), jnp.float32)] * 2,
            pltpu.VMEM((13, nx + 2 * DEEP, ny + 8, nz), jnp.float32),
            pltpu.VMEM((5, nx, ny, nz), jnp.float32),
            pltpu.VMEM((5, nx + 2 * DEEP, ny + 2 * TOP, nz), jnp.float32),
            pltpu.VMEM((STEPS, ny + 8, LANES), jnp.float32),
            pltpu.VMEM((samples, local_rec), jnp.float32),
            pltpu.VMEM((8, LANES), jnp.float32),
            pltpu.VMEM((n * 8, LANES), jnp.float32),
            pltpu.VMEM((2, n_rec // LANES, LANES), jnp.int32),
            pltpu.VMEM((LANES, n_rec), jnp.float32),
            pltpu.VMEM((ny + 8, n_rec), jnp.float32),
            pltpu.VMEM((16 * n + 48 * (nx + 4) * (ny + 4), LANES), jnp.float32),
            pltpu.SemaphoreType.DMA((6,)),
            pltpu.SemaphoreType.DMA((2,)),
            pltpu.SemaphoreType.DMA((8,)),
            pltpu.SemaphoreType.REGULAR((max(n_gx, n_gy, 3) - 2,)),
        ],
        compiler_params=pltpu.CompilerParams(
            collective_id=0, has_side_effects=True, vmem_limit_bytes=48 * 1024 * 1024
        ),
        name="window",
    )(*[pltpu.with_memory_space_constraint(a, pltpu.HBM) for a in (*args[:13], traces, *positions)], segment_start)
    return pl.pallas_call(
        write_out,
        out_shape=(block,) * 3,
        in_specs=[pl.BlockSpec(memory_space=pltpu.VMEM)] * 3,
        out_specs=(pl.BlockSpec(memory_space=pltpu.HBM),) * 3,
        scratch_shapes=[pltpu.SemaphoreType.DMA((3,))],
        compiler_params=pltpu.CompilerParams(vmem_limit_bytes=1024 * 1024),
        name="write_out",
    )(*[pltpu.with_memory_space_constraint(end, pltpu.VMEM) for end in ends])


def solution(mesh):
    block, cell = P(("shot", "gx"), "gy", None), P("gx", "gy", None)
    return jax.shard_map(
        per_device,
        mesh=mesh,
        in_specs=(block,) * 8 + (cell,) * 5 + (P("shot", ("gx", "gy")), P(), P(), P()),
        out_specs=(block,) * 3,
        check_vma=False,
    )
```

```python
import functools

import jax
import jax.numpy as jnp
from jax import lax
from jax.experimental import pallas as pl
from jax.experimental.pallas import tpu as pltpu
from jax.sharding import PartitionSpec as P

STEPS = 4
REC_DEPTH = 4
DEEP = 3
RINGS = (0, 2, 1, 0)
BASE = 8
TOP = 12
LANES = 128
TILE = 8
SIDES = ((0, -1), (0, 1), (-1, 0), (1, 0), (-1, -1), (-1, 1), (1, -1), (1, 1))
MESH = pl.DeviceIdType.MESH
scope = jax.named_scope


def sine(x):
    s = x * x
    c = 1.6059044e-10
    for k in (-2.5052108e-8, 2.7557319e-6, -1.98412698e-4, 8.3333333e-3, -1.66666667e-1):
        c = c * s + k
    return x + x * (s * c)


def cosine(x):
    s = x * x
    c = -1.1470746e-11
    for k in (2.0876757e-9, -2.7557319e-7, 2.4801587e-5, -1.38888889e-3, 4.16666667e-2, -0.5):
        c = c * s + k
    return 1.0 + s * c


def kernel(sizes, *refs):
    n_gx, n_gy, nx, ny, nz, local_rec, n_rec = sizes
    fields, model = refs[:8], refs[8:13]
    traces, rec_x, rec_y, start = refs[13:17]
    image, p_last, q_last = refs[17:20]
    (*held, old_0, old_1, coef, earth, unit, inject, rows, window, gathered, rec_pos, hot_x, hot_y, pool,
     load_sem, send_sem, recv_sem, ready) = refs[20:]
    waves = (held[:STEPS + 1], held[STEPS + 1:])
    olds = (old_0, old_1)
    wide = ny + 8
    n = n_gx * n_gy
    gx, gy = lax.axis_index("gx"), lax.axis_index("gy")
    me = gx * n_gy + gy

    barrier = pltpu.get_barrier_semaphore()

    def peer_id(i):
        peer = lax.rem(me + n - i, n)
        return {"gx": peer // n_gy, "gy": lax.rem(peer, n_gy)}

    def await_rows(sem, count):
        part = pool.at[pl.ds(0, count)]
        pltpu.make_async_copy(part, part, sem).wait()

    inner_x, inner_y = pl.ds(DEEP, nx), pl.ds(TOP, ny)

    with scope("loads"):
        for g in range(2):
            for f in range(2):
                pltpu.make_async_copy(
                    fields[4 * g + 2 * f + 1], waves[g][0].at[f, inner_x, inner_y], load_sem.at[0]
                ).start()
        for i in range(5):
            pltpu.make_async_copy(model[i], earth.at[i], load_sem.at[1]).start()
        load_traces = pltpu.make_async_copy(traces, rows, load_sem.at[2])
        load_traces.start()

    def there(dx, dy):
        ok = None
        for d, pos, count in ((dx, gx, n_gx), (dy, gy, n_gy)):
            if d:
                test = pos + d < count if d > 0 else pos + d >= 0
                ok = test if ok is None else ok & test
        return ok

    def tell_neighbours(sem):
        for dx, dy in SIDES:
            @pl.when(there(dx, dy))
            def _():
                pl.semaphore_signal(
                    sem, inc=1, device_id={"gx": gx + dx, "gy": gy + dy}, device_id_type=MESH
                )

    def count_beside(pos, count):
        return jnp.where(pos > 0, 1, 0) + jnp.where(pos < count - 1, 1, 0)

    neighbours = (1 + count_beside(gx, n_gx)) * (1 + count_beside(gy, n_gy)) - 1
    rounds = max(n_gx, n_gy) - 2

    def hear_neighbours(sem):
        pl.semaphore_wait(sem, neighbours)

    def tell_above(i, carry):
        ahead, peer_x = 1 + i // n_gx, lax.rem(i, n_gx)
        apart = jnp.where(peer_x > gx, peer_x - gx, gx - peer_x)

        @pl.when((gy + ahead < n_gy) & ((ahead > 1) | (apart > 1)))
        def _():
            pl.semaphore_signal(
                barrier, inc=1, device_id={"gx": peer_x, "gy": gy + ahead}, device_id_type=MESH
            )

        return carry

    with scope("greet"):
        tell_neighbours(barrier)
        above = n_gx * (n_gy - 1)
        if above:
            lax.fori_loop(0, above, tell_above, 0, unroll=min(12, above))

    def span(d, start, size, first, last):
        if d == 0:
            return pl.ds(start, size), pl.ds(start, size)
        if d > 0:
            return pl.ds(start + size - last, last - first), pl.ds(start - last, last - first)
        return pl.ds(start + first, last - first), pl.ds(start + size + first, last - first)

    def send(ref, slot, near, far, corner, out=0):
        for dx, dy in SIDES:
            first, last = (0, corner) if dx and dy else (near, far)
            if last == first:
                continue

            @pl.when(there(dx, dy))
            def _():
                src_x, dst_x = span(dx, DEEP, nx, first, last)
                src_y, dst_y = span(dy, TOP, ny, first, last)
                pltpu.make_async_remote_copy(
                    src_ref=ref.at[:, src_x, src_y],
                    dst_ref=ref.at[:, dst_x, dst_y],
                    send_sem=send_sem.at[out],
                    recv_sem=recv_sem.at[slot],
                    device_id={"gx": gx + dx, "gy": gy + dy},
                    device_id_type=MESH,
                ).start()

    def halo_rows(count, layers, corner, beside_x, beside_y):
        faces = beside_x * ny + beside_y * nx
        return count * (layers * faces + beside_x * beside_y * corner * corner)

    def by_place(act):
        for beside_x in range(min(n_gx, 3)):
            for beside_y in range(min(n_gy, 3)):
                here_x = jnp.where(gx > 0, 1, 0) + jnp.where(gx < n_gx - 1, 1, 0) == beside_x
                here_y = jnp.where(gy > 0, 1, 0) + jnp.where(gy < n_gy - 1, 1, 0) == beside_y

                @pl.when(here_x & here_y)
                def _():
                    act(beside_x, beside_y)

    def await_halo(slot, *groups, sems=recv_sem):
        def act(beside_x, beside_y):
            total = sum(halo_rows(*group, beside_x, beside_y) for group in groups)
            if total:
                await_rows(sems.at[slot], total)

        by_place(act)

    with scope("wait_now"):
        await_rows(load_sem.at[0], 4 * nx * ny)
    with scope("barrier"):
        beside = count_beside(gx, n_gx)
        pl.semaphore_wait(barrier, n_gx * gy + beside + jnp.where(gy < n_gy - 1, 1 + beside, 0))
    with scope("send_src0"):
        if rounds > 0:
            tell_neighbours(ready.at[0])
        send(waves[0][0], 0, 0, 1, 2)
        send(waves[1][0], 1, 0, 1, 2)

    per_row = LANES // local_rec
    packed = STEPS // per_row
    with scope("window"):
        load_traces.wait()
        window[...] = jnp.zeros_like(window)
        window[0:STEPS, 0:local_rec] = rows[pl.ds(start[0], STEPS), :]
        sample = window[...]
        for r in range(packed):
            row = sample[r * per_row:r * per_row + 1]
            for j in range(1, per_row):
                row = row + pltpu.roll(sample[r * per_row + j:r * per_row + j + 1], j * local_rec, 1)
            window[r:r + 1] = row
        mine = pl.ds(pl.multiple_of(me * 8, 8), packed)
        gathered[mine] = window[0:packed]

    def far_start(lower, i, carry):
        peer_x, peer_y = i // n_gy, lax.rem(i, n_gy)
        chosen = peer_y < gy if lower else (peer_y >= gy) & (i != me)

        @pl.when(chosen)
        def _():
            pltpu.make_async_remote_copy(
                src_ref=window.at[0:packed],
                dst_ref=gathered.at[mine],
                send_sem=send_sem.at[0],
                recv_sem=recv_sem.at[7],
                device_id={"gx": peer_x, "gy": peer_y},
                device_id_type=MESH,
            ).start()

        return carry

    with scope("far_below"):
        lax.fori_loop(0, n, functools.partial(far_start, True), 0, unroll=min(16, n))

    with scope("wait_model"):
        await_rows(load_sem.at[1], 5 * nx * ny)

    def units(x, carry):
        v = earth[0, x]
        f_e = 1.0 + 2.0 * earth[1, x]
        f_d = jnp.sqrt(1.0 + 2.0 * earth[2, x])
        tilt = earth[3, x]
        half = 0.5 * earth[4, x]
        sin_t = sine(tilt)
        sin_h, cos_h = sine(half), cosine(half)
        sin_a = 2.0 * sin_h * cos_h
        cos_a = 1.0 - 2.0 * sin_h * sin_h
        to = (x + DEEP, inner_y)
        unit[(0, *to)] = v
        unit[(1, *to)] = v * f_e
        unit[(2, *to)] = v * f_d
        unit[(3, *to)] = sin_t * cos_a
        unit[(4, *to)] = sin_t * sin_a
        return carry

    with scope("units"):
        lax.fori_loop(0, nx, units, 0, unroll=nx)

    with scope("send_model"):
        send(unit, 2, 0, 2, 2)
    with scope("send_layer"):
        send(waves[0][0], 3, 1, 2, 0)
        send(waves[1][0], 4, 1, 2, 0)
    for g in range(2):
        for f in range(2):
            pltpu.make_async_copy(
                fields[4 * g + 2 * f], olds[g].at[f, :, pl.ds(TOP - BASE, ny)], load_sem.at[3]
            ).start()
    load_x = pltpu.make_async_copy(rec_x, rec_pos.at[0], load_sem.at[4])
    load_y = pltpu.make_async_copy(rec_y, rec_pos.at[1], load_sem.at[5])
    load_x.start()
    load_y.start()

    with scope("round"):
        if rounds > 0:
            hear_neighbours(ready.at[0])
        if rounds > 1:
            tell_neighbours(ready.at[1])

    def clear(ref, count, depth):
        zeros = jnp.zeros((wide, nz), jnp.float32)
        for edge, first in ((gx == 0, DEEP - depth), (gx == n_gx - 1, DEEP + nx)):
            @pl.when(edge)
            def _():
                for f in range(count):
                    for x in range(first, first + depth):
                        ref[f, x, BASE:BASE + wide] = zeros
        for edge, first in ((gy == 0, TOP - depth), (gy == n_gy - 1, TOP + ny)):
            @pl.when(edge)
            def _():
                for f in range(count):
                    ref[f, :, first:first + depth] = jnp.zeros((nx + 2 * DEEP, depth, nz), jnp.float32)

    with scope("clear"):
        for g in range(2):
            clear(waves[g][0], 2, 2)
            clear(waves[g][1], 2, 3)
        clear(unit, 5, 2)

    def after(value):
        return pltpu.roll(value, nz - 1, 1)

    def before(value):
        return pltpu.roll(value, 1, 1)

    def factors(x, first, count):
        lane = lax.broadcasted_iota(jnp.int32, (count, nz), 1)
        at = pl.ds(first, count)
        to = pl.ds(first - BASE, count)
        n_x, n_y = unit[3, x, at], unit[4, x, at]
        a_xx, a_yy = n_x * n_x, n_y * n_y
        a_zz = 1.0 - (a_xx + a_yy)
        half_z = 0.5 * jnp.sqrt(a_zz)
        a_xz, a_yz = half_z * n_x, half_z * n_y
        coef[0, x, to] = a_xx
        coef[1, x, to] = a_yy
        coef[4, x, to] = 1.0 - a_xx
        coef[5, x, to] = 1.0 - a_yy
        coef[8, x, to] = (0.5 * n_x) * n_y
        for shift, edge, i in ((before, lane == 0, 0), (after, lane == nz - 1, 1)):
            moved = shift(a_zz)
            coef[2 + i, x, to] = jnp.where(edge, 0.0, moved)
            coef[6 + i, x, to] = jnp.where(edge, 0.0, 1.0 - moved)
            coef[9 + 2 * i, x, to] = jnp.where(edge, 0.0, shift(a_xz))
            coef[10 + 2 * i, x, to] = jnp.where(edge, 0.0, shift(a_yz))

    def inner_factors(x, carry):
        factors(x, TOP, ny)
        return carry

    def outer_factors(x, carry):
        factors(x, BASE, 8)
        factors(x, BASE + wide - 8, 8)
        return carry

    with scope("inner_factors"):
        lax.fori_loop(DEEP, DEEP + nx, inner_factors, 0, unroll=nx)

    def around(now, f, x, lo, count):
        center = now[f, x, pl.ds(lo, count)]
        y_up, y_down = now[f, x, pl.ds(lo + 1, count)], now[f, x, pl.ds(lo - 1, count)]
        return center, y_up - y_down, y_up + y_down

    def rotated(planes, x, at, weights):
        sign, w_x, w_y, w_up, w_down = weights
        (x_down, dy_down, _), (center, d_y, s_y), (x_up, dy_up, _) = planes
        d_x, d_xy = x_up - x_down, dy_up - dy_down
        flat = coef[w_x, x, at] * (x_up + x_down) + coef[w_y, x, at] * s_y
        mixed = coef[8, x, at] * d_xy
        above, below = coef[w_up, x, at] * center, coef[w_down, x, at] * center
        mixed_above = coef[9, x, at] * d_x + coef[10, x, at] * d_y
        mixed_below = coef[11, x, at] * d_x + coef[12, x, at] * d_y
        if sign > 0:
            return (flat + mixed) + (after(above + mixed_above) + before(below - mixed_below))
        return (flat - mixed) + (after(above - mixed_above) + before(below + mixed_below))

    def add_range(first, last, lo, count):
        rows_here = pl.ds(lo, count)

        def add_samples(x, carry):
            new = waves[1][1][0, x, rows_here] + samples_at(STEPS - 1, x, lo - BASE, count)
            waves[1][1][0, x, rows_here] = new
            return carry

        lax.fori_loop(first, last, add_samples, 0, unroll=last - first)

    def step(g, level, part=None):
        ring = RINGS[level]
        first, last = DEEP - ring, DEEP + nx + ring
        if part is None:
            plane_range(g, level, first, last, BASE if ring else TOP, wide if ring else ny)
            return
        lo, count, margin = (TOP + 1, ny - 2, 1) if level == 1 else (TOP + 4, ny - 8, 2)
        if part == "inner":
            plane_range(g, level, DEEP + margin, DEEP + nx - margin, lo, count)
        else:
            for edge in ((first, DEEP + margin), (DEEP + nx - margin, last)):
                plane_range(g, level, *edge, BASE, wide)
            for start in (BASE, BASE + wide - 8):
                plane_range(g, level, DEEP + margin, DEEP + nx - margin, start, 8)

    def plane_range(g, level, first, last, lo, count):
        for start in range(lo, lo + count, TILE):
            tile_range(g, level, first, last, start, min(TILE, lo + count - start))

    def tile_range(g, level, first, last, lo, count):
        now, later = waves[g][level], waves[g][level + 1] if g == 0 or level < STEPS - 1 else None
        mid, at = pl.ds(lo, count), pl.ds(lo - BASE, count)

        def plane(x, carry):
            p_planes, q_planes = [[*carry[f], around(now, f, x + 1, lo, count)] for f in range(2)]
            p_now, q_now = p_planes[1][0], q_planes[1][0]
            p_two, q_two = p_now + p_now, q_now + q_now
            across = rotated(p_planes, x, at, (-1, 4, 5, 6, 7)) - (p_two + p_two)
            q_axis = rotated(q_planes, x, at, (1, 0, 1, 2, 3)) - q_two
            v_d = unit[2, x, mid]
            if level:
                p_prev, q_prev = waves[g][level - 1][0, x, mid], waves[g][level - 1][1, x, mid]
            else:
                p_prev, q_prev = olds[g][0, x - DEEP, at], olds[g][1, x - DEEP, at]
            p_next = (p_two - p_prev) + (unit[1, x, mid] * across + v_d * q_axis)
            if g == 1 and level:
                p_next = p_next + samples_at(STEPS - 1 - level, x, lo - BASE, count)
            carry = (tuple(p_planes[1:]), tuple(q_planes[1:]))
            if g == 0 and level == STEPS - 1:
                later[0, x, mid] = p_next
                return carry
            q_next = (q_two - q_prev) + (v_d * across + unit[0, x, mid] * q_axis)
            if g == 1 and level == STEPS - 1:
                to = pl.ds(lo - TOP, count)
                p_last[x - DEEP, to] = p_next
                q_last[x - DEEP, to] = q_next
                total = waves[0][0][0, x, mid] * p_next
                for k in range(STEPS):
                    total = total + waves[1][k][0, x, mid] * waves[0][STEPS - k][0, x, mid]
                image[x - DEEP, to] = total
            else:
                later[0, x, mid] = p_next
                later[1, x, mid] = q_next
            return carry

        begin = tuple(tuple(around(now, f, x, lo, count) for x in (first - 1, first)) for f in range(2))
        lax.fori_loop(first, last, plane, begin, unroll=last - first)

    n_rows = n_rec // LANES
    wide_x = hot_x.shape[0]

    def find(i, carry):
        to = pl.ds(pl.multiple_of(i * LANES, LANES), LANES)
        x_id = lax.broadcasted_iota(jnp.int32, (wide_x, LANES), 0) + (gx * nx - DEEP)
        y_id = lax.broadcasted_iota(jnp.int32, (wide, LANES), 0) + (gy * ny - (TOP - BASE))
        hot_x[:, to] = jnp.where(rec_pos[0, pl.ds(i, 1)] == x_id, 1.0, 0.0)
        hot_y[:, to] = jnp.where(rec_pos[1, pl.ds(i, 1)] == y_id, 1.0, 0.0)
        return carry

    with scope("find"):
        load_x.wait()
        load_y.wait()
        lax.fori_loop(0, n_rows, find, 0, unroll=8)

    def make_planes():
        segment = lax.broadcasted_iota(jnp.int32, (n_rows, LANES), 1) // local_rec
        parts = []
        for k in range(STEPS):
            r, own = k // per_row, k % per_row
            sample = None
            for j in range(per_row):
                piece = gathered[pl.ds(j * 8 + r, n_rows, stride=per_row * 8), :]
                piece = jnp.where(segment == own, piece, 0.0)
                if j != own:
                    piece = pltpu.roll(piece, (j - own) * local_rec % LANES, 1)
                sample = piece if sample is None else sample + piece
            for _ in range(3):
                part = sample.astype(jnp.bfloat16).astype(jnp.float32)
                parts.append(part)
                sample = sample - part
        chunk = min(8, n_rows)
        total = jnp.zeros((3 * STEPS * wide, wide_x), jnp.float32)
        for base in range(0, n_rows, chunk):
            columns = slice(base * LANES, (base + chunk) * LANES)
            left = jnp.concatenate(
                [
                    jnp.concatenate(
                        [hot_y[:, i * LANES:(i + 1) * LANES] * part[i:i + 1] for part in parts], axis=0
                    )
                    for i in range(base, base + chunk)
                ],
                axis=1,
            )
            total = total + lax.dot_general(
                left, hot_x[:, columns], (((1,), (1,)), ((), ())), preferred_element_type=jnp.float32
            )
        for k in range(STEPS):
            three = [total[(3 * k + i) * wide:(3 * k + i + 1) * wide] for i in range(3)]
            inject[k] = (three[0] + three[1]) + three[2]

    def samples_at(k, x, first, count):
        lane = lax.broadcasted_iota(jnp.int32, (count, LANES), 1)
        column = pltpu.roll(inject[k, pl.ds(first, count)], lax.rem(LANES + REC_DEPTH - x, LANES), 1)
        return jnp.where(lane == REC_DEPTH, column, 0.0)

    with scope("rounds"):
        for i in range(1, rounds):
            hear_neighbours(ready.at[i])
            if i + 1 < rounds:
                tell_neighbours(ready.at[i + 1])
    with scope("far_rest"):
        lax.fori_loop(0, n, functools.partial(far_start, False), 0, unroll=min(16, n))
    with scope("wait_prev"):
        await_rows(load_sem.at[3], 4 * nx * ny)
    with scope("wait_src0"):
        await_halo(0, (2, 1, 2))
    with scope("src_step0"):
        step(0, 0)
    with scope("send_src1"):
        send(waves[0][1], 5, 0, 3, 3)
    with scope("wait_rec0"):
        await_halo(1, (2, 1, 2))
    with scope("rec_step0"):
        step(1, 0)
    with scope("send_rec1"):
        send(waves[1][1], 6, 0, 3, 3, out=1)
    with scope("src_inner"):
        for level in (1, 2):
            step(0, level, "inner")
    with scope("wait_model_halo"):
        await_halo(2, (5, 2, 2))
    with scope("outer_factors"):
        lax.fori_loop(DEEP, DEEP + nx, outer_factors, 0, unroll=nx)
        for x in (DEEP - 2, DEEP - 1, DEEP + nx, DEEP + nx + 1):
            factors(x, BASE, wide)
    with scope("wait_far"):
        if n > 1:
            await_rows(recv_sem.at[7], packed * (n - 1))
    with scope("planes"):
        make_planes()
    with scope("rec_inner"):
        await_halo(1, (2, 3, 3), sems=send_sem)
        add_range(DEEP, DEEP + nx, TOP, ny)
        step(1, 1, "inner")
        step(1, 2, "inner")
    with scope("wait_src1"):
        await_halo(3, (2, 1, 0))
        await_halo(5, (2, 3, 3))
    for level in range(1, STEPS):
        with scope("src_step%d" % level):
            step(0, level, "outer" if level < STEPS - 1 else None)
    with scope("wait_rec1"):
        await_halo(4, (2, 1, 0))
        await_halo(6, (2, 3, 3))

    with scope("add_samples"):
        add_range(0, DEEP, BASE, wide)
        add_range(DEEP + nx, nx + 2 * DEEP, BASE, wide)
        for start in (TOP - 4, TOP + ny):
            add_range(DEEP, DEEP + nx, start, 4)

    for level in range(1, STEPS):
        with scope("rec_step%d" % level):
            step(1, level, "outer" if level < STEPS - 1 else None)

    def finish(beside_x, beside_y):
        total = packed * (n - 1)
        for group in ((4, 1, 2), (5, 2, 2), (4, 1, 0), (2, 3, 3)):
            total += halo_rows(*group, beside_x, beside_y)
        if total:
            await_rows(send_sem.at[0], total)

    with scope("finish"):
        by_place(finish)


def write_out(*refs):
    values, results, done = refs[:3], refs[3:6], refs[6]
    copies = [pltpu.make_async_copy(values[i], results[i], done.at[i]) for i in range(3)]
    for copy in copies:
        copy.start()
    for copy in copies:
        copy.wait()


def per_device(*args):
    nx, ny, nz = args[0].shape
    n_gx, n_gy = lax.axis_size("gx"), lax.axis_size("gy")
    traces, receiver_x, receiver_y, segment_start = args[13:]
    samples, local_rec = traces.shape
    n_rec = receiver_x.shape[0]
    n = n_gx * n_gy
    sizes = (n_gx, n_gy, nx, ny, nz, local_rec, n_rec)
    positions = [r.reshape(n_rec // LANES, LANES) for r in (receiver_x, receiver_y)]
    anywhere = pl.BlockSpec(memory_space=pltpu.HBM)
    block = jax.ShapeDtypeStruct((nx, ny, nz), jnp.float32)
    held = pltpu.VMEM((nx, ny, nz), jnp.float32)
    ends = pl.pallas_call(
        functools.partial(kernel, sizes),
        out_shape=(held,) * 3,
        in_specs=[anywhere] * 16 + [pl.BlockSpec(memory_space=pltpu.SMEM)],
        out_specs=(pl.BlockSpec(memory_space=pltpu.VMEM),) * 3,
        scratch_shapes=[
            *[pltpu.VMEM((2, nx + 2 * DEEP, ny + 2 * TOP, nz), jnp.float32)] * (2 * STEPS + 2),
            *[pltpu.VMEM((2, nx, ny + 8, nz), jnp.float32)] * 2,
            pltpu.VMEM((13, nx + 2 * DEEP, ny + 8, nz), jnp.float32),
            pltpu.VMEM((5, nx, ny, nz), jnp.float32),
            pltpu.VMEM((5, nx + 2 * DEEP, ny + 2 * TOP, nz), jnp.float32),
            pltpu.VMEM((STEPS, ny + 8, LANES), jnp.float32),
            pltpu.VMEM((samples, local_rec), jnp.float32),
            pltpu.VMEM((8, LANES), jnp.float32),
            pltpu.VMEM((n * 8, LANES), jnp.float32),
            pltpu.VMEM((2, n_rec // LANES, LANES), jnp.int32),
            pltpu.VMEM((LANES, n_rec), jnp.float32),
            pltpu.VMEM((ny + 8, n_rec), jnp.float32),
            pltpu.VMEM((16 * n + 48 * (nx + 4) * (ny + 4), LANES), jnp.float32),
            pltpu.SemaphoreType.DMA((6,)),
            pltpu.SemaphoreType.DMA((2,)),
            pltpu.SemaphoreType.DMA((8,)),
            pltpu.SemaphoreType.REGULAR((max(n_gx, n_gy, 3) - 2,)),
        ],
        compiler_params=pltpu.CompilerParams(
            collective_id=0, has_side_effects=True, vmem_limit_bytes=48 * 1024 * 1024
        ),
        name="window",
    )(*[pltpu.with_memory_space_constraint(a, pltpu.HBM) for a in (*args[:13], traces, *positions)], segment_start)
    return pl.pallas_call(
        write_out,
        out_shape=(block,) * 3,
        in_specs=[pl.BlockSpec(memory_space=pltpu.VMEM)] * 3,
        out_specs=(pl.BlockSpec(memory_space=pltpu.HBM),) * 3,
        scratch_shapes=[pltpu.SemaphoreType.DMA((3,))],
        compiler_params=pltpu.CompilerParams(vmem_limit_bytes=1024 * 1024),
        name="write_out",
    )(*[pltpu.with_memory_space_constraint(end, pltpu.VMEM) for end in ends])


def solution(mesh):
    block, cell = P(("shot", "gx"), "gy", None), P("gx", "gy", None)
    return jax.shard_map(
        per_device,
        mesh=mesh,
        in_specs=(block,) * 8 + (cell,) * 5 + (P("shot", ("gx", "gy")), P(), P(), P()),
        out_specs=(block,) * 3,
        check_vma=False,
    )
```
